32 devices in a mesh: chan: 8 (over z, x), tm: 4 (over y, core).
Axes of the slice: x: 2, y: 2, z: 4, core: 2. Of those that a mesh axis runs over, the one named last changes fastest.
Arguments:
- volts: bfloat16 [8, 64, 2, 98304], P('chan', None, None, 'tm'), may hold values from -6 to 6
- scales: float32 [8, 64, 384], P('chan', None, 'tm'), may hold values from 0.25 to 4
- dm_rate: int32 [8, 16, 2], replicated, may hold values from 8192 to 16384
Outputs:
- dedispersed: bfloat16 [64, 8, 2, 98304], P('chan', None, None, 'tm')
The draws below stay inside these ranges and needn't reach their ends.
All inputs are finite; a program needn't handle non-finite values.
Results may differ from the reference program's by a relative error of at most 0.0083.
Values may be sent and summed in bfloat16 or wider, within the bound.
A program may use at most 128 MiB of HBM per device.

```python
import math
import jax
import jax.numpy as jnp
from jax import lax

RADIX_A = 128
RADIX_B = 256
NFFT = 32768
INTERSECTION = 8192
SEGMENT = 24576
BLOCK = 256
BEAMS = 16
CHAN_DEV = 2
CHAN_BLOCKS = 8
LANES = 64
TIMES = 98304
NBLOCKS = 384
N_TM = 4


def plant(values, rng, smallest, high):
    shape = values.shape
    index_at = [jax.random.randint(jax.random.fold_in(rng, axis), (), 0, shape[axis]) for axis in range(len(shape))]
    values = values.at[tuple(index_at)].set(smallest)
    longest = shape.index(max(shape))
    index_at[longest] = (index_at[longest] + 1) % shape[longest]
    return values.at[tuple(index_at)].set(high)


def block_scale(stream_key, shape, cuts, low, top_value):
    loudness = 1.0
    for axis_at, shards_of in cuts:
        heights = jax.random.uniform(jax.random.fold_in(jax.random.fold_in(stream_key, 6), axis_at), (shards_of,), jnp.float32, low / len(cuts), top_value / len(cuts))
        loudness = loudness * jnp.repeat(jnp.exp(heights), shape[axis_at] // shards_of).reshape((-1,) + (1,) * (len(shape) - 1 - axis_at))
    return loudness


def gaussian(stream_key, dims, width, most, split=(), kind=jnp.bfloat16):
    drawn = width * jax.random.normal(stream_key, dims, jnp.float32)
    if split:
        drawn = drawn * block_scale(stream_key, dims, split, -0.22, 0.18)
    return jnp.clip(drawn, -most, most).astype(kind)


def setup_inputs(seed: int = 0) -> dict:
    seeds = jax.random.split(jax.random.key(seed), 4)
    return {
        "volts": gaussian(seeds[0], (CHAN_BLOCKS, LANES, 2, TIMES), 1.0, 6.0, ((0, 8), (3, 4))),
        "scales": jnp.clip(jnp.exp(math.log(4.0) - 2.7725887 * jax.random.uniform(seeds[1], (CHAN_BLOCKS, LANES, NBLOCKS), jnp.float32) ** block_scale(seeds[1], (CHAN_BLOCKS, LANES, NBLOCKS), ((0, 8), (2, 4)), -0.2, 0.2)), 0.25, 4.0),
        "dm_rate": plant(jax.random.randint(seeds[2], (CHAN_BLOCKS, BEAMS, CHAN_DEV), INTERSECTION, 2 * INTERSECTION + 1), jax.random.fold_in(seeds[2], 1), INTERSECTION, 2 * INTERSECTION).astype(jnp.int32),
    }


def dft_parts(radix):
    row_index = lax.broadcasted_iota(jnp.int32, (radix, radix), 0)
    col_index = lax.broadcasted_iota(jnp.int32, (radix, radix), 1)
    angle = (2.0 * math.pi / radix) * ((row_index * col_index) % radix).astype(jnp.float32)
    return jnp.cos(angle).astype(jnp.bfloat16), (-jnp.sin(angle)).astype(jnp.bfloat16)


def twiddle_parts():
    length = RADIX_A * RADIX_B
    row_index = lax.broadcasted_iota(jnp.int32, (RADIX_A, RADIX_B), 0)
    col_index = lax.broadcasted_iota(jnp.int32, (RADIX_A, RADIX_B), 1)
    angle = (2.0 * math.pi / length) * ((row_index * col_index) % length).astype(jnp.float32)
    return jnp.cos(angle), -jnp.sin(angle)


def chirp_parts(rates):
    length = RADIX_A * RADIX_B
    row_index = lax.broadcasted_iota(jnp.int32, (RADIX_A, RADIX_B), 0)
    col_index = lax.broadcasted_iota(jnp.int32, (RADIX_A, RADIX_B), 1)
    frequency = row_index + RADIX_A * col_index
    distance = jnp.abs((frequency + length // 2) % length - length // 2)
    upper_part = distance // RADIX_B
    lower_part = distance % RADIX_B
    delay_term = (length - (frequency * (INTERSECTION // 2)) % length) % length
    rate_grid = rates.reshape(-1, 1, 1)
    first_term = (rate_grid * upper_part * upper_part) % (4 * RADIX_A * RADIX_A)
    second_term = (rate_grid * upper_part * lower_part) % (2 * RADIX_A * RADIX_A * RADIX_B)
    third_term = rate_grid * lower_part * lower_part
    turns = first_term.astype(jnp.float32) / (4.0 * RADIX_A * RADIX_A)
    turns = turns + second_term.astype(jnp.float32) / (2.0 * RADIX_A * RADIX_A * RADIX_B)
    turns = turns + third_term.astype(jnp.float32) / (4.0 * length * length)
    turns = turns + delay_term.astype(jnp.float32) / (1.0 * length)
    angle = (2.0 * math.pi) * turns
    return jnp.cos(angle), jnp.sin(angle)


def to_bfloat(values):
    return lax.optimization_barrier(values.astype(jnp.bfloat16)).astype(jnp.float32)


def left_apply(matrix, array):
    return jnp.einsum("kn,snb->skb", matrix, array)


def right_apply(array, matrix):
    return jnp.einsum("skn,nm->skm", array, matrix)


def dedisperse(segments, rates):
    streams = segments.shape[0]
    head_rows = INTERSECTION // RADIX_B
    data = segments.reshape(streams, 2, RADIX_A, RADIX_B).astype(jnp.float32)
    left_re, left_im = dft_parts(RADIX_A)
    right_re, right_im = dft_parts(RADIX_B)
    left_re = left_re.astype(jnp.float32)
    left_im = left_im.astype(jnp.float32)
    right_re = right_re.astype(jnp.float32)
    right_im = right_im.astype(jnp.float32)
    twist_re, twist_im = twiddle_parts()
    real_in, imag_in = data[:, 0], data[:, 1]
    section_re = left_apply(left_re, real_in) - left_apply(left_im, imag_in)
    section_im = left_apply(left_im, real_in) + left_apply(left_re, imag_in)
    turned_re = to_bfloat(section_re * twist_re - section_im * twist_im)
    turned_im = to_bfloat(section_re * twist_im + section_im * twist_re)
    spec_re = right_apply(turned_re, right_re) - right_apply(turned_im, right_im)
    spec_im = right_apply(turned_re, right_im) + right_apply(turned_im, right_re)
    chirp_re, chirp_im = chirp_parts(rates)
    shaped_re = to_bfloat(spec_re * chirp_re - spec_im * chirp_im)
    shaped_im = to_bfloat(spec_re * chirp_im + spec_im * chirp_re)
    back_re = right_apply(shaped_re, right_re) + right_apply(shaped_im, right_im)
    back_im = right_apply(shaped_im, right_re) - right_apply(shaped_re, right_im)
    untwist_re = to_bfloat(back_re * twist_re + back_im * twist_im)
    untwist_im = to_bfloat(back_im * twist_re - back_re * twist_im)
    out_re = left_apply(left_re, untwist_re) + left_apply(left_im, untwist_im)
    out_im = left_apply(left_re, untwist_im) - left_apply(left_im, untwist_re)
    scale_back = 1.0 / (RADIX_A * RADIX_B)
    result = jnp.stack([out_re, out_im], axis=1)[:, :, head_rows:, :] * scale_back
    return result.reshape(streams, 2, SEGMENT).astype(jnp.bfloat16)


def reference(volts, scales, dm_rate):
    rate_table = jnp.repeat(dm_rate.reshape(CHAN_BLOCKS, BEAMS * CHAN_DEV), 2, axis=1)

    def one_lane(lane_index):
        lane_block = lax.dynamic_index_in_dim(volts, lane_index, 1, keepdims=False)
        lane_scales = lax.dynamic_index_in_dim(scales, lane_index, 1, keepdims=False)
        scaled = lane_block.reshape(CHAN_BLOCKS, 2, NBLOCKS, BLOCK).astype(jnp.float32) * lane_scales[:, None, :, None]
        values = scaled.reshape(CHAN_BLOCKS, 2, TIMES).astype(jnp.bfloat16)
        pieces = values.reshape(CHAN_BLOCKS, 2, N_TM, SEGMENT)
        tails = pieces[:, :, :, SEGMENT - INTERSECTION:]
        prior = jnp.concatenate([jnp.zeros_like(tails[:, :, :1]), tails[:, :, :-1]], axis=2)
        joined = jnp.concatenate([prior, pieces], axis=3)
        joined = jnp.transpose(joined, (0, 2, 1, 3)).reshape(CHAN_BLOCKS * N_TM, 2, NFFT)
        lane_rates = lax.dynamic_index_in_dim(rate_table, lane_index, 1, keepdims=False)
        stream_rates = jnp.repeat(lane_rates, N_TM)
        cleaned = dedisperse(joined, stream_rates).reshape(CHAN_BLOCKS, N_TM, 2, SEGMENT)
        return jnp.transpose(cleaned, (0, 2, 1, 3)).reshape(CHAN_BLOCKS, 2, TIMES)

    return lax.map(one_lane, jnp.arange(LANES, dtype=jnp.int32))
```

```python
import functools
import math

import jax
import jax.numpy as jnp
import ml_dtypes
import numpy as np
from jax import lax
from jax.experimental import pallas as pl
from jax.experimental.pallas import tpu as pltpu
from jax.sharding import PartitionSpec as P

RADIX_A = 128
RADIX_B = 256
NFFT = RADIX_A * RADIX_B
INTERSECTION = 8192
LANE = 128
HALVES = RADIX_B // LANE
PRIOR = INTERSECTION // LANE * 2
MESH = pl.DeviceIdType.MESH


def dft_parts(radix):
    index = np.arange(radix)
    angle = 2.0 * np.pi / radix * (np.outer(index, index) % radix)
    rounded = lambda x: x.astype(np.float32).astype(ml_dtypes.bfloat16).astype(np.float32)
    return rounded(np.cos(angle)), rounded(-np.sin(angle))


def tables():
    are, aim = dft_parts(RADIX_A)
    bre, bim = dft_parts(RADIX_B)
    eye = np.eye(HALVES, dtype=np.float32)
    left = np.array([[are, -aim], [aim, are]])
    left = np.einsum("dckn,hg->hdkngc", left, eye).reshape(HALVES * 2 * RADIX_A, -1)
    back = np.array([[are, aim], [-aim, are]]) / NFFT
    back = np.einsum("dcnk,hg->nhdgck", back, eye).reshape(-1, HALVES * 2 * RADIX_A)
    back = back[PRIOR:]
    right = np.array([[bre, bim], [-bim, bre]])
    right = right.transpose(0, 2, 1, 3).reshape(2 * RADIX_B, 2 * RADIX_B)
    unright = np.array([[bre, -bim], [bim, bre]])
    unright = unright.transpose(0, 2, 1, 3).reshape(2 * RADIX_B, 2 * RADIX_B)
    turn = np.outer(np.arange(RADIX_A), np.arange(RADIX_B)) % NFFT
    angle = 2.0 * np.pi / NFFT * turn
    twist = np.stack([np.cos(angle), -np.sin(angle)]).astype(np.float32)
    half = lambda x: x.astype(ml_dtypes.bfloat16)
    return half(left), half(right), half(unright), half(back), twist


def chirp(rate):
    shape = (RADIX_A, RADIX_B)
    k = lax.broadcasted_iota(jnp.int32, shape, 0) + RADIX_A * lax.broadcasted_iota(jnp.int32, shape, 1)
    g = jnp.minimum(k, NFFT - k)
    phase = rate * (g * g) - (k << 29)
    quarter = (phase + (1 << 29)) >> 30
    x = (phase - (quarter << 30)).astype(jnp.float32) * (2.0 * math.pi / 2.0**32)
    y = x * x
    s = x + x * y * (-1.6666654611e-1 + y * (8.3321608736e-3 + y * -1.9515295891e-4))
    c = 1.0 + y * (-0.5 + y * (4.166664568298827e-2 + y * (-1.388731625493765e-3 + y * 2.443315711809948e-5)))
    odd = (quarter & 1) == 1
    re = jnp.where(odd, s, c)
    im = jnp.where(odd, c, s)
    re = jnp.where(((quarter + 1) & 2) == 2, -re, re)
    im = jnp.where((quarter & 2) == 2, -im, im)
    return re, im


def filtered(segments, cre, cim, left, right, unright, back, twist):
    wre, wim = twist[0], twist[1]
    section = jnp.dot(left[...], segments, preferred_element_type=jnp.float32)
    ups = []
    for s in range(segments.shape[1] // LANE):
        cols = slice(s * LANE, (s + 1) * LANE)
        part = lambda d: jnp.concatenate(
            [section[(h * 2 + d) * RADIX_A : (h * 2 + d + 1) * RADIX_A, cols] for h in range(HALVES)], axis=1
        )
        sre, sim = part(0), part(1)
        turned = jnp.concatenate(
            [(sre * wre - sim * wim).astype(jnp.bfloat16), (sre * wim + sim * wre).astype(jnp.bfloat16)], axis=1
        )
        spec = jnp.dot(turned, right[...], preferred_element_type=jnp.float32)
        sre, sim = spec[:, :RADIX_B], spec[:, RADIX_B:]
        shaped = jnp.concatenate(
            [(sre * cre - sim * cim).astype(jnp.bfloat16), (sre * cim + sim * cre).astype(jnp.bfloat16)], axis=1
        )
        spun = jnp.dot(shaped, unright[...], preferred_element_type=jnp.float32)
        sre, sim = spun[:, :RADIX_B], spun[:, RADIX_B:]
        ure = (sre * wre + sim * wim).astype(jnp.bfloat16)
        uim = (sim * wre - sre * wim).astype(jnp.bfloat16)
        pieces = []
        for h in range(HALVES):
            pieces += [ure[:, h * LANE : (h + 1) * LANE], uim[:, h * LANE : (h + 1) * LANE]]
        ups.append(jnp.concatenate(pieces, axis=0))
    return jnp.dot(
        back[...], jnp.concatenate(ups, axis=1), preferred_element_type=jnp.float32
    ).astype(jnp.bfloat16)


def bitwise_xor(a, b, bits):
    total = 0
    for i in range(bits):
        total = total + (a // 2**i + b // 2**i) % 2 * 2**i
    return total


def staggered(b, groups):
    last = 2 * groups - 1
    far = 1 - (1 - (b + last) // (last + 1)) - b % 2 + b // last
    return far, (b + 1) // 2 - far


def kernel(n, n_tm, own, width, early, rates, scales, volts, left_in, right_in, unright_in, back_in, twist_in,
           out, late, late_chirp, left, right, unright, back, twist,
           got, tail, gains, prior_gains, square, spread,
           own_sem, table_sem, gain_send, gain_recv, prior_send, prior_recv, tail_send, tail_recv,
           body_send, body_recv, next_send, next_recv, ready):
    me = lax.axis_index("chan")
    tm = lax.axis_index("tm")
    groups = own // width
    items = n * groups
    half = n // 2
    rows = volts.shape[1]
    count = scales.shape[2]
    bits = (n - 1).bit_length()
    root = n - 1
    across = n - 2
    xor = lambda r: bitwise_xor(me, r, bits)
    has_next = tm < n_tm - 1

    def signal(sem, peer):
        pl.semaphore_signal(sem, inc=1, device_id={"chan": peer}, device_id_type=MESH)

    def remote(src, dst, send, recv, device_id):
        return pltpu.make_async_remote_copy(
            src_ref=src, dst_ref=dst, send_sem=send, recv_sem=recv, device_id=device_id, device_id_type=MESH
        )

    def send_tail(g, r):
        peer = xor(r)
        cut = pl.ds(rows - PRIOR, PRIOR)
        return remote(
            volts.at[pl.ds(peer * own + g * width, width), cut], got.at[me, pl.ds(g * width, width), cut],
            tail_send.at[g * n + r], tail_recv.at[g * n + r], {"chan": peer},
        )

    def send_body(g, r):
        peer = xor(r)
        cut = pl.ds(0, rows - PRIOR)
        return remote(
            volts.at[pl.ds(peer * own + g * width, width), cut], got.at[me, pl.ds(g * width, width), cut],
            body_send.at[g * n + r], body_recv.at[g * n + r], {"chan": peer},
        )

    def send_gain(r):
        peer = xor(r)
        return remote(scales.at[peer], gains.at[me], gain_send.at[r], gain_recv.at[r], {"chan": peer})

    def forward_gains():
        return remote(gains, prior_gains, prior_send.at[0], prior_recv.at[0], {"tm": tm + 1})

    def forward(g, r):
        peer = xor(r)
        lanes = pl.ds(g * width, width)
        return remote(
            got.at[peer, lanes, pl.ds(rows - PRIOR, PRIOR)], tail.at[peer, lanes],
            next_send.at[g * n + r], next_recv.at[g * n + r], {"tm": tm + 1},
        )

    def own_item(g):
        lanes = pl.ds(g * width, width)
        return pltpu.make_async_copy(volts.at[pl.ds(me * own + g * width, width)], got.at[me, lanes], own_sem.at[g])

    own_gain = pltpu.make_async_copy(scales.at[me], gains.at[me], own_sem.at[groups])
    fills = [
        pltpu.make_async_copy(src, dst, table_sem.at[j])
        for j, (src, dst) in enumerate(
            [(left_in, left), (twist_in, twist), (right_in, right), (unright_in, unright), (back_in, back)]
        )
    ]

    barrier = pltpu.get_barrier_semaphore()
    signal(barrier, xor(across))

    @pl.when(tm > 0)
    def _():
        pl.semaphore_signal(barrier, inc=1, device_id={"tm": tm - 1}, device_id_type=MESH)

    @pl.when(me < root)
    def _():
        signal(barrier, root)

    followed = 1 - (tm + 1) // n_tm
    pl.semaphore_wait(barrier, 1 + followed + (me + 1) // n * (n - 1))

    @pl.when(me == root)
    def _():
        @pl.loop(1, n)
        def _(r):
            signal(ready, bitwise_xor(root, r, bits))

    def send(q, r):
        far, g = staggered(q, groups)

        @pl.when(far == 0)
        def _():
            send_tail(g, r).start()

        @pl.when(far == 1)
        def _():
            send_body(g, r).start()

    @pl.loop(0, early)
    def _(q):
        send(q, across)

    own_gain.start()

    @pl.loop(0, groups)
    def _(g):
        own_item(g).start()

    @pl.when(me < root)
    def _():
        pl.semaphore_wait(ready, 1)

    @pl.loop(1, n)
    def _(r):
        send_gain(r).start()

    @pl.loop(0, 2 * groups * (n - 1))
    def _(i):
        q, j = i // (n - 1), i % (n - 1) + 1
        r = j % 2 * half + j // 2

        @pl.when(jnp.logical_or(r != across, q >= early))
        def _():
            send(q, r)

    for fill in fills:
        fill.start()

    @pl.when(tm == 0)
    def _():
        prior_gains[...] = jnp.zeros_like(prior_gains)

        @pl.loop(0, n)
        def _(c):
            tail[c] = jnp.zeros(tail.shape[1:], tail.dtype)

    own_gain.wait()

    @pl.loop(1, n)
    def _(r):
        send_gain(r).wait_recv()

    @pl.when(has_next)
    def _():
        forward_gains().start()

    @pl.loop(0, groups)
    def _(g):
        own_item(g).wait()

    def advance(g, r):
        @pl.when(r > 0)
        def _():
            send_tail(g, r).wait_recv()

        @pl.when(has_next)
        def _():
            forward(g, r).start()

    @pl.loop(0, half)
    def _(i):
        advance(0, i)

    per = rows // count
    square[...] = jnp.zeros_like(square)

    def gather(src):
        for c in range(n):
            square[c * own : (c + 1) * own, 0:count] = src[c]
        return square[...].T

    turned = gather(gains)[0:count]
    for j in range(per):
        spread[pl.ds(PRIOR + j, count, stride=per), :] = turned

    @pl.when(tm > 0)
    def _():
        forward_gains().wait_recv()

    turned = gather(prior_gains)[count - PRIOR // per : count]
    for j in range(per):
        spread[pl.ds(j, PRIOR // per, stride=per), :] = turned

    for fill in fills:
        fill.wait()

    def place(i):
        far, g = staggered(i // half, groups)
        return g, far * half + i % half

    def arrive(i):
        g, r = place(i)

        @pl.when(r > 0)
        def _():
            send_body(g, r).wait_recv()

        @pl.when(tm > 0)
        def _():
            forward(g, r).wait_recv()

    def segments(i):
        g, r = place(i)
        c, base = xor(r), g * width
        first = c * own + base
        rolled = pltpu.roll(spread[...], (LANE - first) % LANE, 1)
        streams = []
        for s in range(width):
            gain = jnp.broadcast_to(rolled[:, s : s + 1], rolled.shape)
            raw = jnp.concatenate([tail[c, base + s], got[c, base + s]], axis=0)
            streams.append((raw.astype(jnp.float32) * gain).astype(jnp.bfloat16))
        return jnp.concatenate(streams, axis=1)

    def rotation(i):
        g, r = place(i)
        lane = me * own + g * width
        return chirp(rates[xor(r), lane // 2 % 2, lane // 4])

    @pl.loop(0, items - 1)
    def _(i):
        g, r = place(i)

        @pl.when(i + half < items)
        def _():
            advance(*place(i + half))

        arrive(i)
        cre, cim = rotation(i)
        result = filtered(segments(i), cre, cim, left, right, unright, back, twist)
        for s in range(width):
            out[g * width + s, xor(r)] = result[:, s * LANE : (s + 1) * LANE]

    late_chirp[0], late_chirp[1] = rotation(items - 1)

    @pl.loop(0, items)
    def _(i):
        g, r = i // n, i % n

        @pl.when(r > 0)
        def _():
            send_tail(g, r).wait_send()
            send_body(g, r).wait_send()

        @pl.when(has_next)
        def _():
            forward(g, r).wait_send()

    @pl.loop(1, n)
    def _(r):
        send_gain(r).wait_send()

    @pl.when(has_next)
    def _():
        forward_gains().wait_send()

    arrive(items - 1)
    late[...] = segments(items - 1)


def settle(n, own, width, src, late, late_chirp, left, right, unright, back, twist, out, last, bulk_sem, side_sem, last_sem):
    c = bitwise_xor(lax.axis_index("chan"), n - 1, (n - 1).bit_length())
    base = own - width
    bulk = [pltpu.make_async_copy(src.at[q], out.at[q], bulk_sem.at[q]) for q in range(base)]

    def side(s, j):
        peer = (c + j) % n
        return pltpu.make_async_copy(src.at[base + s, peer], out.at[base + s, peer], side_sem.at[s * n + j])

    for copy in bulk:
        copy.start()
    for s in range(width):

        @pl.loop(1, n)
        def _(j):
            side(s, j).start()

    result = filtered(late[...], late_chirp[0], late_chirp[1], left, right, unright, back, twist)
    final = []
    for s in range(width):
        last[s] = result[:, s * LANE : (s + 1) * LANE]
        final.append(pltpu.make_async_copy(last.at[s], out.at[base + s, c], last_sem.at[s]))
        final[s].start()
    for s in range(width):

        @pl.loop(1, n)
        def _(j):
            side(s, j).wait()

    for copy in bulk + final:
        copy.wait()


def body(volts, scales, dm_rate):
    lanes, seg_len = volts.shape[1], volts.shape[3]
    count = scales.shape[2]
    n, n_tm = lax.axis_size("chan"), lax.axis_size("tm")
    own = lanes // n
    width = 2 if own % 2 == 0 else 1
    rows = seg_len // LANE * 2
    values = volts.reshape(lanes, 2, seg_len // LANE, LANE).transpose(0, 2, 1, 3).reshape(lanes, rows, LANE)
    consts = tables()
    groups = own // width
    items = n * groups
    early = min(3, 2 * groups)
    vmem = pl.BlockSpec(memory_space=pltpu.VMEM)
    hbm = pl.BlockSpec(memory_space=pltpu.MemorySpace.HBM)
    dma = pltpu.SemaphoreType.DMA
    bf16, f32 = jnp.bfloat16, jnp.float32
    kept = pl.pallas_call(
        functools.partial(kernel, n, n_tm, own, width, early),
        out_shape=[
            pltpu.VMEM((own, n, rows, LANE), bf16),
            pltpu.VMEM((PRIOR + rows, width * LANE), bf16),
            pltpu.VMEM((2, RADIX_A, RADIX_B), f32),
        ]
        + [pltpu.VMEM(x.shape, x.dtype) for x in consts],
        in_specs=[pl.BlockSpec(memory_space=pltpu.SMEM)] + [hbm] * 7,
        out_specs=[vmem] * 8,
        scratch_shapes=[
            pltpu.VMEM((n, own, rows, LANE), bf16),
            pltpu.VMEM((n, own, PRIOR, LANE), bf16),
            pltpu.VMEM((n, own, count), f32),
            pltpu.VMEM((n, own, count), f32),
            pltpu.VMEM((LANE, LANE), f32),
            pltpu.VMEM((PRIOR + rows, LANE), f32),
            dma((groups + 1,)),
            dma((5,)),
            dma((n,)),
            dma((n,)),
            dma((1,)),
            dma((1,)),
        ]
        + [dma((items,))] * 6
        + [pltpu.SemaphoreType.REGULAR],
        compiler_params=pltpu.CompilerParams(
            collective_id=0, has_side_effects=True, vmem_limit_bytes=52 * 2**20
        ),
        name="dedisperse",
    )(dm_rate.transpose(0, 2, 1), scales.reshape(n, own, count), values, *consts)
    out = pl.pallas_call(
        functools.partial(settle, n, own, width),
        out_shape=jax.ShapeDtypeStruct((own, n, rows, LANE), bf16),
        in_specs=[vmem] * 8,
        out_specs=hbm,
        scratch_shapes=[
            pltpu.VMEM((width, rows, LANE), bf16),
            dma((max(own - width, 1),)),
            dma((width * n,)),
            dma((width,)),
        ],
        compiler_params=pltpu.CompilerParams(vmem_limit_bytes=16 * 2**20),
        name="settle",
    )(*kept)
    out = out.reshape(own, n, seg_len // LANE, 2, LANE).transpose(0, 1, 3, 2, 4)
    return out.reshape(own, n, 2, seg_len)


def solution(mesh):
    return jax.shard_map(
        body,
        mesh=mesh,
        in_specs=(P("chan", None, None, "tm"), P("chan", None, "tm"), P()),
        out_specs=P("chan", None, None, "tm"),
        check_vma=False,
    )
```

```python
import functools
import math

import jax
import jax.numpy as jnp
import ml_dtypes
import numpy as np
from jax import lax
from jax.experimental import pallas as pl
from jax.experimental.pallas import tpu as pltpu
from jax.sharding import PartitionSpec as P

RADIX_A = 128
RADIX_B = 256
NFFT = RADIX_A * RADIX_B
INTERSECTION = 8192
LANE = 128
HALVES = RADIX_B // LANE
PRIOR = INTERSECTION // LANE * 2
MESH = pl.DeviceIdType.MESH


def dft_parts(radix):
    index = np.arange(radix)
    angle = 2.0 * np.pi / radix * (np.outer(index, index) % radix)
    rounded = lambda x: x.astype(np.float32).astype(ml_dtypes.bfloat16).astype(np.float32)
    return rounded(np.cos(angle)), rounded(-np.sin(angle))


def tables():
    are, aim = dft_parts(RADIX_A)
    bre, bim = dft_parts(RADIX_B)
    eye = np.eye(HALVES, dtype=np.float32)
    left = np.array([[are, -aim], [aim, are]])
    left = np.einsum("dckn,hg->hdkngc", left, eye).reshape(HALVES * 2 * RADIX_A, -1)
    back = np.array([[are, aim], [-aim, are]]) / NFFT
    back = np.einsum("dcnk,hg->nhdgck", back, eye).reshape(-1, HALVES * 2 * RADIX_A)
    back = back[PRIOR:]
    right = np.array([[bre, bim], [-bim, bre]])
    right = right.transpose(0, 2, 1, 3).reshape(2 * RADIX_B, 2 * RADIX_B)
    unright = np.array([[bre, -bim], [bim, bre]])
    unright = unright.transpose(0, 2, 1, 3).reshape(2 * RADIX_B, 2 * RADIX_B)
    turn = np.outer(np.arange(RADIX_A), np.arange(RADIX_B)) % NFFT
    angle = 2.0 * np.pi / NFFT * turn
    twist = np.stack([np.cos(angle), -np.sin(angle)]).astype(np.float32)
    half = lambda x: x.astype(ml_dtypes.bfloat16)
    return half(left), half(right), half(unright), half(back), twist


def chirp(rate):
    shape = (RADIX_A, RADIX_B)
    k = lax.broadcasted_iota(jnp.int32, shape, 0) + RADIX_A * lax.broadcasted_iota(jnp.int32, shape, 1)
    g = jnp.minimum(k, NFFT - k)
    phase = rate * (g * g) - (k << 29)
    quarter = (phase + (1 << 29)) >> 30
    x = (phase - (quarter << 30)).astype(jnp.float32) * (2.0 * math.pi / 2.0**32)
    y = x * x
    s = x + x * y * (-1.6666654611e-1 + y * (8.3321608736e-3 + y * -1.9515295891e-4))
    c = 1.0 + y * (-0.5 + y * (4.166664568298827e-2 + y * (-1.388731625493765e-3 + y * 2.443315711809948e-5)))
    odd = (quarter & 1) == 1
    re = jnp.where(odd, s, c)
    im = jnp.where(odd, c, s)
    re = jnp.where(((quarter + 1) & 2) == 2, -re, re)
    im = jnp.where((quarter & 2) == 2, -im, im)
    return re, im


def filtered(segments, cre, cim, left, right, unright, back, twist):
    wre, wim = twist[0], twist[1]
    section = jnp.dot(left[...], segments, preferred_element_type=jnp.float32)
    ups = []
    for s in range(segments.shape[1] // LANE):
        cols = slice(s * LANE, (s + 1) * LANE)
        part = lambda d: jnp.concatenate(
            [section[(h * 2 + d) * RADIX_A : (h * 2 + d + 1) * RADIX_A, cols] for h in range(HALVES)], axis=1
        )
        sre, sim = part(0), part(1)
        turned = jnp.concatenate(
            [(sre * wre - sim * wim).astype(jnp.bfloat16), (sre * wim + sim * wre).astype(jnp.bfloat16)], axis=1
        )
        spec = jnp.dot(turned, right[...], preferred_element_type=jnp.float32)
        sre, sim = spec[:, :RADIX_B], spec[:, RADIX_B:]
        shaped = jnp.concatenate(
            [(sre * cre - sim * cim).astype(jnp.bfloat16), (sre * cim + sim * cre).astype(jnp.bfloat16)], axis=1
        )
        spun = jnp.dot(shaped, unright[...], preferred_element_type=jnp.float32)
        sre, sim = spun[:, :RADIX_B], spun[:, RADIX_B:]
        ure = (sre * wre + sim * wim).astype(jnp.bfloat16)
        uim = (sim * wre - sre * wim).astype(jnp.bfloat16)
        pieces = []
        for h in range(HALVES):
            pieces += [ure[:, h * LANE : (h + 1) * LANE], uim[:, h * LANE : (h + 1) * LANE]]
        ups.append(jnp.concatenate(pieces, axis=0))
    return jnp.dot(
        back[...], jnp.concatenate(ups, axis=1), preferred_element_type=jnp.float32
    ).astype(jnp.bfloat16)


def bitwise_xor(a, b, bits):
    total = 0
    for i in range(bits):
        total = total + (a // 2**i + b // 2**i) % 2 * 2**i
    return total


def staggered(b, groups):
    last = 2 * groups - 1
    far = 1 - (1 - (b + last) // (last + 1)) - b % 2 + b // last
    return far, (b + 1) // 2 - far


def turned_order(me, k, n):
    half = n // 2
    outer = 1 - (me // half + me // max(half // 2, 1)) % 2
    return half + (k + half // 2 * outer) % half


def kernel(n, n_tm, own, width, early, rates_in, scales, volts, left_in, right_in, unright_in, back_in, twist_in,
           out, late, late_chirp, left, right, unright, back, twist,
           got, tail, gains, prior_gains, square, spread,
           own_sem, table_sem, gain_send, gain_recv, prior_send, prior_recv, tail_send, tail_recv,
           body_send, body_recv, next_send, next_recv, ready, rates):
    me = lax.axis_index("chan")
    tm = lax.axis_index("tm")
    groups = own // width
    items = n * groups
    half = n // 2
    rows = volts.shape[1]
    count = scales.shape[2]
    bits = (n - 1).bit_length()
    root = n - 1
    across = n - 2
    xor = lambda r: bitwise_xor(me, r, bits)
    has_next = tm < n_tm - 1

    def signal(sem, peer):
        pl.semaphore_signal(sem, inc=1, device_id={"chan": peer}, device_id_type=MESH)

    def remote(src, dst, send, recv, device_id):
        return pltpu.make_async_remote_copy(
            src_ref=src, dst_ref=dst, send_sem=send, recv_sem=recv, device_id=device_id, device_id_type=MESH
        )

    def send_tail(g, r):
        peer = xor(r)
        cut = pl.ds(rows - PRIOR, PRIOR)
        return remote(
            volts.at[pl.ds(peer * own + g * width, width), cut], got.at[me, pl.ds(g * width, width), cut],
            tail_send.at[g * n + r], tail_recv.at[g * n + r], {"chan": peer},
        )

    def send_body(g, r):
        peer = xor(r)
        cut = pl.ds(0, rows - PRIOR)
        return remote(
            volts.at[pl.ds(peer * own + g * width, width), cut], got.at[me, pl.ds(g * width, width), cut],
            body_send.at[g * n + r], body_recv.at[g * n + r], {"chan": peer},
        )

    def send_gain(r):
        peer = xor(r)
        return remote(scales.at[peer], gains.at[me], gain_send.at[r], gain_recv.at[r], {"chan": peer})

    def forward_gains():
        return remote(gains, prior_gains, prior_send.at[0], prior_recv.at[0], {"tm": tm + 1})

    def forward(g, r):
        peer = xor(r)
        lanes = pl.ds(g * width, width)
        return remote(
            got.at[peer, lanes, pl.ds(rows - PRIOR, PRIOR)], tail.at[peer, lanes],
            next_send.at[g * n + r], next_recv.at[g * n + r], {"tm": tm + 1},
        )

    def own_item(g):
        lanes = pl.ds(g * width, width)
        return pltpu.make_async_copy(volts.at[pl.ds(me * own + g * width, width)], got.at[me, lanes], own_sem.at[g])

    own_gain = pltpu.make_async_copy(scales.at[me], gains.at[me], own_sem.at[groups])
    fills = [
        pltpu.make_async_copy(src, dst, table_sem.at[j])
        for j, (src, dst) in enumerate(
            [(rates_in, rates), (left_in, left), (twist_in, twist), (right_in, right), (unright_in, unright), (back_in, back)]
        )
    ]

    barrier = pltpu.get_barrier_semaphore()
    is_root = me == root
    signal(barrier, xor(across))

    @pl.when(me < root)
    def _():
        signal(barrier, root)

    followed, preceded = 1 - (tm + 1) // n_tm, 1 - (n_tm - tm) // n_tm

    @pl.when(jnp.logical_and(is_root, tm > 0))
    def _():
        pl.semaphore_signal(barrier, inc=1, device_id={"tm": tm - 1}, device_id_type=MESH)

    @pl.when(jnp.logical_and(is_root, has_next))
    def _():
        pl.semaphore_signal(barrier, inc=1, device_id={"tm": tm + 1}, device_id_type=MESH)

    pl.semaphore_wait(barrier, 1 + (me + 1) // n * (n - 1 + followed + preceded))

    def release(k):
        @pl.loop(1, n)
        def _(r):
            signal(ready.at[k], bitwise_xor(root, r, bits))

    @pl.when(is_root)
    def _():
        release(0)

    @pl.when(jnp.logical_and(is_root, tm > 0))
    def _():
        pl.semaphore_signal(ready.at[2], inc=1, device_id={"tm": tm - 1}, device_id_type=MESH)

    def send(q, r):
        far, g = staggered(q, groups)
        (send_body if far else send_tail)(g, r).start()

    for q in range(early):
        send(q, across)

    own_gain.start()

    @pl.loop(0, groups)
    def _(g):
        own_item(g).start()

    @pl.when(me < root)
    def _():
        pl.semaphore_wait(ready.at[0], 1)

    @pl.loop(1, n)
    def _(r):
        send_gain(r).start()

    for q in range(2 * groups):
        for j in range(1, n):
            r = j % 2 * half + j // 2
            if r != across or q >= early:
                send(q, r)

    for fill in fills:
        fill.start()

    @pl.when(tm == 0)
    def _():
        prior_gains[...] = jnp.zeros_like(prior_gains)

        @pl.loop(0, n)
        def _(c):
            tail[c] = jnp.zeros(tail.shape[1:], tail.dtype)

    @pl.when(jnp.logical_and(is_root, has_next))
    def _():
        pl.semaphore_wait(ready.at[2], 1)

    @pl.when(jnp.logical_and(is_root, has_next))
    def _():
        release(1)

    @pl.when(jnp.logical_and(me < root, has_next))
    def _():
        pl.semaphore_wait(ready.at[1], 1)

    own_gain.wait()

    @pl.loop(1, n)
    def _(r):
        send_gain(r).wait_recv()

    @pl.when(has_next)
    def _():
        forward_gains().start()

    @pl.loop(0, groups)
    def _(g):
        own_item(g).wait()

    def advance(g, r):
        @pl.when(r > 0)
        def _():
            send_tail(g, r).wait_recv()

        @pl.when(has_next)
        def _():
            forward(g, r).start()

    @pl.loop(0, half)
    def _(i):
        advance(0, i)

    per = rows // count
    square[...] = jnp.zeros_like(square)

    def gather(src):
        for c in range(n):
            square[c * own : (c + 1) * own, 0:count] = src[c]
        return square[...].T

    turned = gather(gains)[0:count]
    for j in range(per):
        spread[pl.ds(PRIOR + j, count, stride=per), :] = turned

    @pl.when(tm > 0)
    def _():
        forward_gains().wait_recv()

    turned = gather(prior_gains)[count - PRIOR // per : count]
    for j in range(per):
        spread[pl.ds(j, PRIOR // per, stride=per), :] = turned

    for fill in fills:
        fill.wait()

    def place(i):
        far, g = staggered(i // half, groups)
        k = i % half
        return g, k + far * (turned_order(me, k, n) - k)

    def arrive(i):
        g, r = place(i)

        @pl.when(r > 0)
        def _():
            send_body(g, r).wait_recv()

        @pl.when(tm > 0)
        def _():
            forward(g, r).wait_recv()

    def segments(i):
        g, r = place(i)
        c, base = xor(r), g * width
        first = c * own + base
        rolled = pltpu.roll(spread[...], (LANE - first) % LANE, 1)
        streams = []
        for s in range(width):
            gain = jnp.broadcast_to(rolled[:, s : s + 1], rolled.shape)
            raw = jnp.concatenate([tail[c, base + s], got[c, base + s]], axis=0)
            streams.append((raw.astype(jnp.float32) * gain).astype(jnp.bfloat16))
        return jnp.concatenate(streams, axis=1)

    def rotation(i):
        g, r = place(i)
        lane = me * own + g * width
        return chirp(rates[xor(r), lane // 2 % 2, lane // 4])

    def settled():
        @pl.loop(0, items)
        def _(i):
            g, r = i // n, i % n

            @pl.when(r > 0)
            def _():
                send_tail(g, r).wait_send()

            @pl.when(jnp.logical_and(r > 0, g < groups - 1))
            def _():
                send_body(g, r).wait_send()

            @pl.when(has_next)
            def _():
                forward(g, r).wait_send()

        @pl.loop(1, n)
        def _(r):
            send_gain(r).wait_send()

        @pl.when(has_next)
        def _():
            forward_gains().wait_send()

    @pl.loop(0, items - 1)
    def _(i):
        g, r = place(i)

        @pl.when(i + half < items)
        def _():
            advance(*place(i + half))

        @pl.when(i == items - 2)
        def _():
            settled()

        arrive(i)
        cre, cim = rotation(i)
        result = filtered(segments(i), cre, cim, left, right, unright, back, twist)
        for s in range(width):
            out[g * width + s, xor(r)] = result[:, s * LANE : (s + 1) * LANE]

    late_chirp[0], late_chirp[1] = rotation(items - 1)

    @pl.loop(1, n)
    def _(r):
        send_body(groups - 1, r).wait_send()

    arrive(items - 1)
    late[...] = segments(items - 1)


def settle(n, own, width, src, late, late_chirp, left, right, unright, back, twist, out, last, bulk_sem, side_sem, last_sem):
    me = lax.axis_index("chan")
    c = bitwise_xor(me, turned_order(me, n // 2 - 1, n), (n - 1).bit_length())
    base = own - width
    bulk = [pltpu.make_async_copy(src.at[q], out.at[q], bulk_sem.at[q]) for q in range(base)]

    def side(s, j):
        peer = (c + j) % n
        return pltpu.make_async_copy(src.at[base + s, peer], out.at[base + s, peer], side_sem.at[s * n + j])

    for copy in bulk:
        copy.start()
    for s in range(width):

        @pl.loop(1, n)
        def _(j):
            side(s, j).start()

    result = filtered(late[...], late_chirp[0], late_chirp[1], left, right, unright, back, twist)
    final = []
    for s in range(width):
        last[s] = result[:, s * LANE : (s + 1) * LANE]
        final.append(pltpu.make_async_copy(last.at[s], out.at[base + s, c], last_sem.at[s]))
        final[s].start()
    for s in range(width):

        @pl.loop(1, n)
        def _(j):
            side(s, j).wait()

    for copy in bulk + final:
        copy.wait()


def body(volts, scales, dm_rate):
    lanes, seg_len = volts.shape[1], volts.shape[3]
    count = scales.shape[2]
    n, n_tm = lax.axis_size("chan"), lax.axis_size("tm")
    own = lanes // n
    width = 2 if own % 2 == 0 else 1
    rows = seg_len // LANE * 2
    values = volts.reshape(lanes, 2, seg_len // LANE, LANE).transpose(0, 2, 1, 3).reshape(lanes, rows, LANE)
    consts = tables()
    groups = own // width
    items = n * groups
    early = min(3, 2 * groups)
    vmem = pl.BlockSpec(memory_space=pltpu.VMEM)
    hbm = pl.BlockSpec(memory_space=pltpu.MemorySpace.HBM)
    dma = pltpu.SemaphoreType.DMA
    bf16, f32 = jnp.bfloat16, jnp.float32
    kept = pl.pallas_call(
        functools.partial(kernel, n, n_tm, own, width, early),
        out_shape=[
            pltpu.VMEM((own, n, rows, LANE), bf16),
            pltpu.VMEM((PRIOR + rows, width * LANE), bf16),
            pltpu.VMEM((2, RADIX_A, RADIX_B), f32),
        ]
        + [pltpu.VMEM(x.shape, x.dtype) for x in consts],
        in_specs=[hbm] * 8,
        out_specs=[vmem] * 8,
        scratch_shapes=[
            pltpu.VMEM((n, own, rows, LANE), bf16),
            pltpu.VMEM((n, own, PRIOR, LANE), bf16),
            pltpu.VMEM((n, own, count), f32),
            pltpu.VMEM((n, own, count), f32),
            pltpu.VMEM((LANE, LANE), f32),
            pltpu.VMEM((PRIOR + rows, LANE), f32),
            dma((groups + 1,)),
            dma((6,)),
            dma((n,)),
            dma((n,)),
            dma((1,)),
            dma((1,)),
        ]
        + [dma((items,))] * 6
        + [pltpu.SemaphoreType.REGULAR((3,)), pltpu.SMEM((n, 2, lanes // 4), jnp.int32)],
        compiler_params=pltpu.CompilerParams(
            collective_id=0, has_side_effects=True, vmem_limit_bytes=52 * 2**20
        ),
        name="dedisperse",
    )(dm_rate.transpose(0, 2, 1), scales.reshape(n, own, count), values, *consts)
    out = pl.pallas_call(
        functools.partial(settle, n, own, width),
        out_shape=jax.ShapeDtypeStruct((own, n, rows, LANE), bf16),
        in_specs=[vmem] * 8,
        out_specs=hbm,
        scratch_shapes=[
            pltpu.VMEM((width, rows, LANE), bf16),
            dma((max(own - width, 1),)),
            dma((width * n,)),
            dma((width,)),
        ],
        compiler_params=pltpu.CompilerParams(vmem_limit_bytes=16 * 2**20),
        name="settle",
    )(*kept)
    out = out.reshape(own, n, seg_len // LANE, 2, LANE).transpose(0, 1, 3, 2, 4)
    return out.reshape(own, n, 2, seg_len)


def solution(mesh):
    return jax.shard_map(
        body,
        mesh=mesh,
        in_specs=(P("chan", None, None, "tm"), P("chan", None, "tm"), P()),
        out_specs=P("chan", None, None, "tm"),
        check_vma=False,
    )
```

```python
import functools
import math

import jax
import jax.numpy as jnp
import ml_dtypes
import numpy as np
from jax import lax
from jax.experimental import pallas as pl
from jax.experimental.pallas import tpu as pltpu
from jax.sharding import PartitionSpec as P

RADIX_A = 128
RADIX_B = 256
NFFT = RADIX_A * RADIX_B
INTERSECTION = 8192
LANE = 128
HALVES = RADIX_B // LANE
PRIOR = INTERSECTION // LANE * 2
MESH = pl.DeviceIdType.MESH


def dft_parts(radix):
    index = np.arange(radix)
    angle = 2.0 * np.pi / radix * (np.outer(index, index) % radix)
    rounded = lambda x: x.astype(np.float32).astype(ml_dtypes.bfloat16).astype(np.float32)
    return rounded(np.cos(angle)), rounded(-np.sin(angle))


def tables():
    are, aim = dft_parts(RADIX_A)
    bre, bim = dft_parts(RADIX_B)
    eye = np.eye(HALVES, dtype=np.float32)
    left = np.array([[are, -aim], [aim, are]])
    left = np.einsum("dckn,hg->hdkngc", left, eye).reshape(HALVES * 2 * RADIX_A, -1)
    back = np.array([[are, aim], [-aim, are]]) / NFFT
    back = np.einsum("dcnk,hg->nhdgck", back, eye).reshape(-1, HALVES * 2 * RADIX_A)
    back = back[PRIOR:]
    right = np.array([[bre, bim], [-bim, bre]])
    right = right.transpose(0, 2, 1, 3).reshape(2 * RADIX_B, 2 * RADIX_B)
    unright = np.array([[bre, -bim], [bim, bre]])
    unright = unright.transpose(0, 2, 1, 3).reshape(2 * RADIX_B, 2 * RADIX_B)
    turn = np.outer(np.arange(RADIX_A), np.arange(RADIX_B)) % NFFT
    angle = 2.0 * np.pi / NFFT * turn
    twist = np.stack([np.cos(angle), -np.sin(angle)]).astype(np.float32)
    half = lambda x: x.astype(ml_dtypes.bfloat16)
    return half(left), half(right), half(unright), half(back), twist


def chirp(rate):
    shape = (RADIX_A, RADIX_B)
    k = lax.broadcasted_iota(jnp.int32, shape, 0) + RADIX_A * lax.broadcasted_iota(jnp.int32, shape, 1)
    g = jnp.minimum(k, NFFT - k)
    phase = rate * (g * g) - (k << 29)
    quarter = (phase + (1 << 29)) >> 30
    x = (phase - (quarter << 30)).astype(jnp.float32) * (2.0 * math.pi / 2.0**32)
    y = x * x
    s = x + x * y * (-1.6666654611e-1 + y * (8.3321608736e-3 + y * -1.9515295891e-4))
    c = 1.0 + y * (-0.5 + y * (4.166664568298827e-2 + y * (-1.388731625493765e-3 + y * 2.443315711809948e-5)))
    odd = (quarter & 1) == 1
    re = jnp.where(odd, s, c)
    im = jnp.where(odd, c, s)
    re = jnp.where(((quarter + 1) & 2) == 2, -re, re)
    im = jnp.where((quarter & 2) == 2, -im, im)
    return re, im


def filtered(segments, cre, cim, left, right, unright, back, twist):
    wre, wim = twist[0], twist[1]
    section = jnp.dot(left[...], segments, preferred_element_type=jnp.float32)
    ups = []
    for s in range(segments.shape[1] // LANE):
        cols = slice(s * LANE, (s + 1) * LANE)
        part = lambda d: jnp.concatenate(
            [section[(h * 2 + d) * RADIX_A : (h * 2 + d + 1) * RADIX_A, cols] for h in range(HALVES)], axis=1
        )
        sre, sim = part(0), part(1)
        turned = jnp.concatenate(
            [(sre * wre - sim * wim).astype(jnp.bfloat16), (sre * wim + sim * wre).astype(jnp.bfloat16)], axis=1
        )
        spec = jnp.dot(turned, right[...], preferred_element_type=jnp.float32)
        sre, sim = spec[:, :RADIX_B], spec[:, RADIX_B:]
        shaped = jnp.concatenate(
            [(sre * cre - sim * cim).astype(jnp.bfloat16), (sre * cim + sim * cre).astype(jnp.bfloat16)], axis=1
        )
        spun = jnp.dot(shaped, unright[...], preferred_element_type=jnp.float32)
        sre, sim = spun[:, :RADIX_B], spun[:, RADIX_B:]
        ure = (sre * wre + sim * wim).astype(jnp.bfloat16)
        uim = (sim * wre - sre * wim).astype(jnp.bfloat16)
        pieces = []
        for h in range(HALVES):
            pieces += [ure[:, h * LANE : (h + 1) * LANE], uim[:, h * LANE : (h + 1) * LANE]]
        ups.append(jnp.concatenate(pieces, axis=0))
    return jnp.dot(
        back[...], jnp.concatenate(ups, axis=1), preferred_element_type=jnp.float32
    ).astype(jnp.bfloat16)


def bitwise_xor(a, b, bits):
    total = 0
    for i in range(bits):
        total = total + (a // 2**i + b // 2**i) % 2 * 2**i
    return total


def parts(groups):
    if groups > 2:
        return [(0, groups - 2), (groups - 2, 2)], [(g, 1) for g in range(groups)]
    return [(0, groups)], [(g, 1) for g in range(groups)]


def staggered(b, groups):
    last = 2 * groups - 1
    far = 1 - (1 - (b + last) // (last + 1)) - b % 2 + b // last
    return far, (b + 1) // 2 - far


def turned_order(me, k, n):
    half = n // 2
    outer = 1 - (me // half + me // max(half // 2, 1)) % 2
    return half + (k + half // 2 * outer) % half


def kernel(n, n_tm, own, width, early, rates_in, scales, volts, left_in, right_in, unright_in, back_in, twist_in,
           out, late, late_gain, late_chirp, left, right, unright, back, twist,
           got, tail, local_scales, mine, gains, prior_gains, square, spread,
           own_sem, table_sem, gain_send, gain_recv, prior_send, prior_recv, tail_send, tail_recv,
           body_send, body_recv, next_send, next_recv, ready, rates):
    me = lax.axis_index("chan")
    tm = lax.axis_index("tm")
    groups = own // width
    items = n * groups
    half = n // 2
    rows = volts.shape[1]
    count = scales.shape[2]
    bits = (n - 1).bit_length()
    root = n - 1
    across = n - 2
    xor = lambda r: bitwise_xor(me, r, bits)
    has_next = tm < n_tm - 1

    def signal(sem, peer):
        pl.semaphore_signal(sem, inc=1, device_id={"chan": peer}, device_id_type=MESH)

    def remote(src, dst, send, recv, device_id):
        return pltpu.make_async_remote_copy(
            src_ref=src, dst_ref=dst, send_sem=send, recv_sem=recv, device_id=device_id, device_id_type=MESH
        )

    tails, bodies = parts(groups)

    def send_tail(p, r):
        peer = xor(r)
        lane, lanes = tails[p][0] * width, tails[p][1] * width
        cut = pl.ds(rows - PRIOR, PRIOR)
        return remote(
            volts.at[pl.ds(peer * own + lane, lanes), cut], got.at[me, pl.ds(lane, lanes), cut],
            tail_send.at[p * n + r], tail_recv.at[p * n + r], {"chan": peer},
        )

    def send_body(p, r):
        peer = xor(r)
        lane, lanes = bodies[p][0] * width, bodies[p][1] * width
        cut = pl.ds(0, rows - PRIOR)
        return remote(
            volts.at[pl.ds(peer * own + lane, lanes), cut], got.at[me, pl.ds(lane, lanes), cut],
            body_send.at[p * n + r], body_recv.at[p * n + r], {"chan": peer},
        )

    def send_gain(r):
        peer = xor(r)
        return remote(mine.at[peer], gains.at[me], gain_send.at[r], gain_recv.at[r], {"chan": peer})

    def forward_gains():
        return remote(gains, prior_gains, prior_send.at[0], prior_recv.at[0], {"tm": tm + 1})

    def forward(p, r):
        peer = xor(r)
        lanes = pl.ds(tails[p][0] * width, tails[p][1] * width)
        return remote(
            got.at[peer, lanes, pl.ds(rows - PRIOR, PRIOR)], tail.at[peer, lanes],
            next_send.at[p * n + r], next_recv.at[p * n + r], {"tm": tm + 1},
        )

    own_items = pltpu.make_async_copy(volts.at[pl.ds(me * own, own)], got.at[me], own_sem.at[0])
    own_gains = pltpu.make_async_copy(scales, local_scales, own_sem.at[1])
    fills = [
        pltpu.make_async_copy(src, dst, table_sem.at[j])
        for j, (src, dst) in enumerate(
            [(rates_in, rates), (left_in, left), (twist_in, twist), (right_in, right), (unright_in, unright), (back_in, back)]
        )
    ]

    barrier = pltpu.get_barrier_semaphore()
    is_root = me == root
    signal(barrier, xor(across))

    @pl.when(me < root)
    def _():
        signal(barrier, root)

    own_gains.start()
    followed, preceded = 1 - (tm + 1) // n_tm, 1 - (n_tm - tm) // n_tm

    @pl.when(jnp.logical_and(is_root, tm > 0))
    def _():
        pl.semaphore_signal(barrier, inc=1, device_id={"tm": tm - 1}, device_id_type=MESH)

    @pl.when(jnp.logical_and(is_root, has_next))
    def _():
        pl.semaphore_signal(barrier, inc=1, device_id={"tm": tm + 1}, device_id_type=MESH)

    pl.semaphore_wait(barrier, 1 + (me + 1) // n * (n - 1 + followed + preceded))

    def release(k):
        @pl.loop(1, n)
        def _(r):
            signal(ready.at[k], bitwise_xor(root, r, bits))

    @pl.when(is_root)
    def _():
        release(0)

    @pl.when(jnp.logical_and(is_root, tm > 0))
    def _():
        pl.semaphore_signal(ready.at[2], inc=1, device_id={"tm": tm - 1}, device_id_type=MESH)

    copies = [(send_tail, 0)] + [(send_body, p) for p in range(len(bodies))]
    copies[3:3] = [(send_tail, p) for p in range(1, len(tails))]

    for send, p in copies[:early]:
        send(p, across).start()

    @pl.when(me < root)
    def _():
        pl.semaphore_wait(ready.at[0], 1)

    for q, (send, p) in enumerate(copies):
        for j in range(1, n):
            r = j % 2 * half + j // 2
            if r != across or q >= early:
                send(p, r).start()
        if q == 0:
            own_gains.wait()
            mine[...] = jnp.zeros_like(mine)
            mine[:, :, 0:count] = local_scales[...]
            for r in range(1, n):
                send_gain(r).start()

    own_items.start()
    for fill in fills:
        fill.start()

    @pl.when(tm == 0)
    def _():
        prior_gains[...] = jnp.zeros_like(prior_gains)

        @pl.loop(0, n)
        def _(c):
            tail[c] = jnp.zeros(tail.shape[1:], tail.dtype)

    @pl.when(jnp.logical_and(is_root, has_next))
    def _():
        pl.semaphore_wait(ready.at[2], 1)

    @pl.when(jnp.logical_and(is_root, has_next))
    def _():
        release(1)

    @pl.when(jnp.logical_and(me < root, has_next))
    def _():
        pl.semaphore_wait(ready.at[1], 1)

    gains[me] = mine[me]

    @pl.loop(1, n)
    def _(r):
        send_gain(r).wait_recv()

    @pl.when(has_next)
    def _():
        forward_gains().start()

    own_items.wait()

    def advance(g, r):
        for p in range(len(tails)):

            @pl.when(jnp.logical_and(g == tails[p][0], r > 0))
            def _():
                send_tail(p, r).wait_recv()

            @pl.when(jnp.logical_and(g == tails[p][0], has_next))
            def _():
                forward(p, r).start()

    @pl.loop(0, half)
    def _(i):
        advance(0, i)

    per = rows // count
    square[...] = jnp.zeros_like(square)

    def gather(src):
        for c in range(n):
            square[c * own : (c + 1) * own] = src[c]
        return square[...].T

    turned = gather(gains)[0:count]
    for j in range(per):
        spread[pl.ds(PRIOR + j, count, stride=per), :] = turned

    @pl.when(tm > 0)
    def _():
        forward_gains().wait_recv()

    turned = gather(prior_gains)[count - PRIOR // per : count]
    for j in range(per):
        spread[pl.ds(j, PRIOR // per, stride=per), :] = turned

    for fill in fills:
        fill.wait()

    def place(i):
        far, g = staggered(i // half, groups)
        k = i % half
        return g, k + far * (turned_order(me, k, n) - k)

    def arrive(i):
        g, r = place(i)
        for p in range(len(tails)):

            @pl.when(jnp.logical_and(g == tails[p][0], tm > 0))
            def _():
                forward(p, r).wait_recv()

        for p in range(len(bodies)):

            @pl.when(jnp.logical_and(g == bodies[p][0], r > 0))
            def _():
                send_body(p, r).wait_recv()

    def stream_gains(first):
        rolled = pltpu.roll(spread[...], (LANE - first) % LANE, 1)
        return [jnp.broadcast_to(rolled[:, s : s + 1], rolled.shape) for s in range(width)]

    def segments(i):
        g, r = place(i)
        c, base = xor(r), g * width
        gain = stream_gains(c * own + base)
        streams = []
        for s in range(width):
            raw = jnp.concatenate([tail[c, base + s], got[c, base + s]], axis=0)
            streams.append((raw.astype(jnp.float32) * gain[s]).astype(jnp.bfloat16))
        return jnp.concatenate(streams, axis=1)

    def rotation(i):
        g, r = place(i)
        lane = me * own + g * width
        return chirp(rates[xor(r), lane // 2 % 2, lane // 4])

    def settled():
        @pl.loop(1, n)
        def _(r):
            for send, p in copies[:-1]:
                send(p, r).wait_send()

        @pl.when(has_next)
        def _():
            @pl.loop(0, n)
            def _(r):
                for p in range(len(tails)):
                    forward(p, r).wait_send()

        @pl.loop(1, n)
        def _(r):
            send_gain(r).wait_send()

        @pl.when(has_next)
        def _():
            forward_gains().wait_send()

    @pl.loop(0, items - 1)
    def _(i):
        g, r = place(i)

        @pl.when(i + half < items)
        def _():
            advance(*place(i + half))

        @pl.when(i == items - 2)
        def _():
            settled()

        arrive(i)
        cre, cim = rotation(i)
        result = filtered(segments(i), cre, cim, left, right, unright, back, twist)
        for s in range(width):
            out[g * width + s, xor(r)] = result[:, s * LANE : (s + 1) * LANE]

    late_chirp[0], late_chirp[1] = rotation(items - 1)

    g, r = place(items - 1)
    c, base = xor(r), g * width
    gain = stream_gains(c * own + base)
    for s in range(width):
        cols = slice(s * LANE, (s + 1) * LANE)
        late_gain[:, cols] = gain[s]

    @pl.loop(1, n)
    def _(r):
        send_body(len(bodies) - 1, r).wait_send()

    arrive(items - 1)
    for s in range(width):
        cols = slice(s * LANE, (s + 1) * LANE)
        late[0:PRIOR, cols] = tail[c, base + s]
        late[PRIOR:, cols] = got[c, base + s]


def settle(n, own, width, src, late, late_gain, late_chirp, left, right, unright, back, twist, out, last, bulk_sem, side_sem, last_sem):
    me = lax.axis_index("chan")
    c = bitwise_xor(me, turned_order(me, n // 2 - 1, n), (n - 1).bit_length())
    base = own - width
    bulk = [pltpu.make_async_copy(src.at[q], out.at[q], bulk_sem.at[q]) for q in range(base)]

    def side(s, j):
        peer = (c + j) % n
        return pltpu.make_async_copy(src.at[base + s, peer], out.at[base + s, peer], side_sem.at[s * n + j])

    for copy in bulk:
        copy.start()
    for s in range(width):

        @pl.loop(1, n)
        def _(j):
            side(s, j).start()

    segments = (late[...].astype(jnp.float32) * late_gain[...]).astype(jnp.bfloat16)
    result = filtered(segments, late_chirp[0], late_chirp[1], left, right, unright, back, twist)
    final = []
    for s in range(width):
        last[s] = result[:, s * LANE : (s + 1) * LANE]
        final.append(pltpu.make_async_copy(last.at[s], out.at[base + s, c], last_sem.at[s]))
        final[s].start()
    for s in range(width):

        @pl.loop(1, n)
        def _(j):
            side(s, j).wait()

    for copy in bulk + final:
        copy.wait()


def body(volts, scales, dm_rate):
    lanes, seg_len = volts.shape[1], volts.shape[3]
    count = scales.shape[2]
    n, n_tm = lax.axis_size("chan"), lax.axis_size("tm")
    own = lanes // n
    width = 2 if own % 2 == 0 else 1
    rows = seg_len // LANE * 2
    values = volts.reshape(lanes, 2, seg_len // LANE, LANE).transpose(0, 2, 1, 3).reshape(lanes, rows, LANE)
    consts = tables()
    groups = own // width
    items = n * groups
    early = 2
    vmem = pl.BlockSpec(memory_space=pltpu.VMEM)
    hbm = pl.BlockSpec(memory_space=pltpu.MemorySpace.HBM)
    dma = pltpu.SemaphoreType.DMA
    bf16, f32 = jnp.bfloat16, jnp.float32
    kept = pl.pallas_call(
        functools.partial(kernel, n, n_tm, own, width, early),
        out_shape=[
            pltpu.VMEM((own, n, rows, LANE), bf16),
            pltpu.VMEM((PRIOR + rows, width * LANE), bf16),
            pltpu.VMEM((PRIOR + rows, width * LANE), f32),
            pltpu.VMEM((2, RADIX_A, RADIX_B), f32),
        ]
        + [pltpu.VMEM(x.shape, x.dtype) for x in consts],
        in_specs=[hbm] * 8,
        out_specs=[vmem] * 9,
        scratch_shapes=[
            pltpu.VMEM((n, own, rows, LANE), bf16),
            pltpu.VMEM((n, own, PRIOR, LANE), bf16),
            pltpu.VMEM((n, own, count), f32),
            pltpu.VMEM((n, own, LANE), f32),
            pltpu.VMEM((n, own, LANE), f32),
            pltpu.VMEM((n, own, LANE), f32),
            pltpu.VMEM((LANE, LANE), f32),
            pltpu.VMEM((PRIOR + rows, LANE), f32),
            dma((2,)),
            dma((6,)),
            dma((n,)),
            dma((n,)),
            dma((1,)),
            dma((1,)),
        ]
        + [dma((items,))] * 6
        + [pltpu.SemaphoreType.REGULAR((3,)), pltpu.SMEM((n, 2, lanes // 4), jnp.int32)],
        compiler_params=pltpu.CompilerParams(
            collective_id=0, has_side_effects=True, vmem_limit_bytes=52 * 2**20
        ),
        name="dedisperse",
    )(dm_rate.transpose(0, 2, 1), scales.reshape(n, own, count), values, *consts)
    out = pl.pallas_call(
        functools.partial(settle, n, own, width),
        out_shape=jax.ShapeDtypeStruct((own, n, rows, LANE), bf16),
        in_specs=[vmem] * 9,
        out_specs=hbm,
        scratch_shapes=[
            pltpu.VMEM((width, rows, LANE), bf16),
            dma((max(own - width, 1),)),
            dma((width * n,)),
            dma((width,)),
        ],
        compiler_params=pltpu.CompilerParams(vmem_limit_bytes=16 * 2**20),
        name="settle",
    )(*kept)
    out = out.reshape(own, n, seg_len // LANE, 2, LANE).transpose(0, 1, 3, 2, 4)
    return out.reshape(own, n, 2, seg_len)


def solution(mesh):
    return jax.shard_map(
        body,
        mesh=mesh,
        in_specs=(P("chan", None, None, "tm"), P("chan", None, "tm"), P()),
        out_specs=P("chan", None, None, "tm"),
        check_vma=False,
    )
```

```python
import functools
import math

import jax
import jax.numpy as jnp
import ml_dtypes
import numpy as np
from jax import lax
from jax.experimental import pallas as pl
from jax.experimental.pallas import tpu as pltpu
from jax.sharding import PartitionSpec as P

RADIX_A = 128
RADIX_B = 256
NFFT = RADIX_A * RADIX_B
INTERSECTION = 8192
LANE = 128
HALVES = RADIX_B // LANE
PRIOR = INTERSECTION // LANE * 2
MESH = pl.DeviceIdType.MESH


def dft_parts(radix):
    index = np.arange(radix)
    angle = 2.0 * np.pi / radix * (np.outer(index, index) % radix)
    rounded = lambda x: x.astype(np.float32).astype(ml_dtypes.bfloat16).astype(np.float32)
    return rounded(np.cos(angle)), rounded(-np.sin(angle))


def tables():
    are, aim = dft_parts(RADIX_A)
    bre, bim = dft_parts(RADIX_B)
    eye = np.eye(HALVES, dtype=np.float32)
    left = np.array([[are, -aim], [aim, are]])
    left = np.einsum("dckn,hg->hdkngc", left, eye).reshape(HALVES * 2 * RADIX_A, -1)
    back = np.array([[are, aim], [-aim, are]]) / NFFT
    back = np.einsum("dcnk,hg->nhdgck", back, eye).reshape(-1, HALVES * 2 * RADIX_A)
    back = back[PRIOR:]
    right = np.array([[bre, bim], [-bim, bre]])
    right = right.transpose(0, 2, 1, 3).reshape(2 * RADIX_B, 2 * RADIX_B)
    unright = np.array([[bre, -bim], [bim, bre]])
    unright = unright.transpose(0, 2, 1, 3).reshape(2 * RADIX_B, 2 * RADIX_B)
    turn = np.outer(np.arange(RADIX_A), np.arange(RADIX_B)) % NFFT
    angle = 2.0 * np.pi / NFFT * turn
    twist = np.stack([np.cos(angle), -np.sin(angle)]).astype(np.float32)
    half = lambda x: x.astype(ml_dtypes.bfloat16)
    return half(left), half(right), half(unright), half(back), twist


def chirp(rate):
    shape = (RADIX_A, RADIX_B)
    k = lax.broadcasted_iota(jnp.int32, shape, 0) + RADIX_A * lax.broadcasted_iota(jnp.int32, shape, 1)
    g = jnp.minimum(k, NFFT - k)
    phase = rate * (g * g) - (k << 29)
    quarter = (phase + (1 << 29)) >> 30
    x = (phase - (quarter << 30)).astype(jnp.float32) * (2.0 * math.pi / 2.0**32)
    y = x * x
    s = x + x * y * (-1.6666654611e-1 + y * (8.3321608736e-3 + y * -1.9515295891e-4))
    c = 1.0 + y * (-0.5 + y * (4.166664568298827e-2 + y * (-1.388731625493765e-3 + y * 2.443315711809948e-5)))
    odd = (quarter & 1) == 1
    re = jnp.where(odd, s, c)
    im = jnp.where(odd, c, s)
    re = jnp.where(((quarter + 1) & 2) == 2, -re, re)
    im = jnp.where((quarter & 2) == 2, -im, im)
    return re, im


def filtered(segments, cre, cim, left, right, unright, back, twist):
    wre, wim = twist[0], twist[1]
    section = jnp.dot(left[...], segments, preferred_element_type=jnp.float32)
    ups = []
    for s in range(segments.shape[1] // LANE):
        cols = slice(s * LANE, (s + 1) * LANE)
        part = lambda d: jnp.concatenate(
            [section[(h * 2 + d) * RADIX_A : (h * 2 + d + 1) * RADIX_A, cols] for h in range(HALVES)], axis=1
        )
        sre, sim = part(0), part(1)
        turned = jnp.concatenate(
            [(sre * wre - sim * wim).astype(jnp.bfloat16), (sre * wim + sim * wre).astype(jnp.bfloat16)], axis=1
        )
        spec = jnp.dot(turned, right[...], preferred_element_type=jnp.float32)
        sre, sim = spec[:, :RADIX_B], spec[:, RADIX_B:]
        shaped = jnp.concatenate(
            [(sre * cre - sim * cim).astype(jnp.bfloat16), (sre * cim + sim * cre).astype(jnp.bfloat16)], axis=1
        )
        spun = jnp.dot(shaped, unright[...], preferred_element_type=jnp.float32)
        sre, sim = spun[:, :RADIX_B], spun[:, RADIX_B:]
        ure = (sre * wre + sim * wim).astype(jnp.bfloat16)
        uim = (sim * wre - sre * wim).astype(jnp.bfloat16)
        pieces = []
        for h in range(HALVES):
            pieces += [ure[:, h * LANE : (h + 1) * LANE], uim[:, h * LANE : (h + 1) * LANE]]
        ups.append(jnp.concatenate(pieces, axis=0))
    return jnp.dot(
        back[...], jnp.concatenate(ups, axis=1), preferred_element_type=jnp.float32
    ).astype(jnp.bfloat16)


def bitwise_xor(a, b, bits):
    total = 0
    for i in range(bits):
        total = total + (a // 2**i + b // 2**i) % 2 * 2**i
    return total


def parts(groups):
    if groups > 2:
        return [(0, groups - 2), (groups - 2, 2)], [(g, 1) for g in range(groups)]
    return [(0, groups)], [(g, 1) for g in range(groups)]


def staggered(b, groups):
    last = 2 * groups - 1
    far = 1 - (1 - (b + last) // (last + 1)) - b % 2 + b // last
    return far, (b + 1) // 2 - far


def turned_order(me, k, n):
    half = n // 2
    outer = 1 - (me // half + me // max(half // 2, 1)) % 2
    return half + (k + half // 2 * outer) % half


def kernel(n, n_tm, own, width, early, rates_in, scales, volts, left_in, right_in, unright_in, back_in, twist_in,
           out, late, late_gain, late_chirp, left, right, unright, back, twist,
           got, tail, local_scales, mine, gains, prior_gains, square, spread,
           own_sem, table_sem, gain_send, gain_recv, prior_send, prior_recv, tail_send, tail_recv,
           body_send, body_recv, next_send, next_recv, ready, rates):
    me = lax.axis_index("chan")
    tm = lax.axis_index("tm")
    groups = own // width
    items = n * groups
    half = n // 2
    rows = volts.shape[1]
    count = scales.shape[2]
    bits = (n - 1).bit_length()
    root = n - 1
    across = n - 2
    xor = lambda r: bitwise_xor(me, r, bits)
    has_next = tm < n_tm - 1

    def signal(sem, peer):
        pl.semaphore_signal(sem, inc=1, device_id={"chan": peer}, device_id_type=MESH)

    def remote(src, dst, send, recv, device_id):
        return pltpu.make_async_remote_copy(
            src_ref=src, dst_ref=dst, send_sem=send, recv_sem=recv, device_id=device_id, device_id_type=MESH
        )

    tails, bodies = parts(groups)

    def send_tail(p, r):
        peer = xor(r)
        lane, lanes = tails[p][0] * width, tails[p][1] * width
        cut = pl.ds(rows - PRIOR, PRIOR)
        return remote(
            volts.at[pl.ds(peer * own + lane, lanes), cut], got.at[me, pl.ds(lane, lanes), cut],
            tail_send.at[p * n + r], tail_recv.at[p * n + r], {"chan": peer},
        )

    def send_body(p, r):
        peer = xor(r)
        lane, lanes = bodies[p][0] * width, bodies[p][1] * width
        cut = pl.ds(0, rows - PRIOR)
        return remote(
            volts.at[pl.ds(peer * own + lane, lanes), cut], got.at[me, pl.ds(lane, lanes), cut],
            body_send.at[p * n + r], body_recv.at[p * n + r], {"chan": peer},
        )

    def send_gain(r):
        peer = xor(r)
        return remote(mine.at[peer], gains.at[me], gain_send.at[r], gain_recv.at[r], {"chan": peer})

    def forward_gains():
        return remote(gains, prior_gains, prior_send.at[0], prior_recv.at[0], {"tm": tm + 1})

    def forward(p, r):
        peer = xor(r)
        lanes = pl.ds(tails[p][0] * width, tails[p][1] * width)
        return remote(
            got.at[peer, lanes, pl.ds(rows - PRIOR, PRIOR)], tail.at[peer, lanes],
            next_send.at[p * n + r], next_recv.at[p * n + r], {"tm": tm + 1},
        )

    own_items = pltpu.make_async_copy(volts.at[pl.ds(me * own, own)], got.at[me], own_sem.at[0])
    own_gains = pltpu.make_async_copy(scales, local_scales, own_sem.at[1])
    fills = [
        pltpu.make_async_copy(src, dst, table_sem.at[j])
        for j, (src, dst) in enumerate(
            [(rates_in, rates), (left_in, left), (twist_in, twist), (right_in, right), (unright_in, unright), (back_in, back)]
        )
    ]

    barrier = pltpu.get_barrier_semaphore()
    is_root = me == root
    signal(barrier, xor(across))

    @pl.when(me < root)
    def _():
        signal(barrier, root)

    own_gains.start()
    followed, preceded = 1 - (tm + 1) // n_tm, 1 - (n_tm - tm) // n_tm

    @pl.when(jnp.logical_and(is_root, tm > 0))
    def _():
        pl.semaphore_signal(barrier, inc=1, device_id={"tm": tm - 1}, device_id_type=MESH)

    @pl.when(jnp.logical_and(is_root, has_next))
    def _():
        pl.semaphore_signal(barrier, inc=1, device_id={"tm": tm + 1}, device_id_type=MESH)

    pl.semaphore_wait(barrier, 1 + (me + 1) // n * (n - 1 + followed + preceded))

    def release(k):
        @pl.loop(1, n)
        def _(r):
            signal(ready.at[k], bitwise_xor(root, r, bits))

    @pl.when(is_root)
    def _():
        release(0)

    @pl.when(jnp.logical_and(is_root, tm > 0))
    def _():
        pl.semaphore_signal(ready.at[2], inc=1, device_id={"tm": tm - 1}, device_id_type=MESH)

    copies = [(send_tail, 0)] + [(send_body, p) for p in range(len(bodies))]
    copies[3:3] = [(send_tail, p) for p in range(1, len(tails))]

    for send, p in copies[:early]:
        send(p, across).start()

    @pl.when(me < root)
    def _():
        pl.semaphore_wait(ready.at[0], 1)

    for q, (send, p) in enumerate(copies):
        for j in range(1, n):
            r = (j + half - 2) % (n - 1) + 1
            if r != across or q >= early:
                send(p, r).start()
        if q == 0:
            own_gains.wait()
            mine[...] = jnp.zeros_like(mine)
            mine[:, :, 0:count] = local_scales[...]
            for r in range(1, n):
                send_gain(r).start()

    own_items.start()
    for fill in fills:
        fill.start()

    @pl.when(tm == 0)
    def _():
        prior_gains[...] = jnp.zeros_like(prior_gains)

        @pl.loop(0, n)
        def _(c):
            tail[c] = jnp.zeros(tail.shape[1:], tail.dtype)

    @pl.when(jnp.logical_and(is_root, has_next))
    def _():
        pl.semaphore_wait(ready.at[2], 1)

    @pl.when(jnp.logical_and(is_root, has_next))
    def _():
        release(1)

    @pl.when(jnp.logical_and(me < root, has_next))
    def _():
        pl.semaphore_wait(ready.at[1], 1)

    gains[me] = mine[me]

    @pl.loop(1, n)
    def _(r):
        send_gain(r).wait_recv()

    @pl.when(has_next)
    def _():
        forward_gains().start()

    own_items.wait()

    def advance(g, r):
        for p in range(len(tails)):

            @pl.when(jnp.logical_and(g == tails[p][0], r > 0))
            def _():
                send_tail(p, r).wait_recv()

            @pl.when(jnp.logical_and(g == tails[p][0], has_next))
            def _():
                forward(p, r).start()

    @pl.loop(0, half)
    def _(i):
        advance(0, i)

    per = rows // count
    square[...] = jnp.zeros_like(square)

    def gather(src):
        for c in range(n):
            square[c * own : (c + 1) * own] = src[c]
        return square[...].T

    turned = gather(gains)[0:count]
    for j in range(per):
        spread[pl.ds(PRIOR + j, count, stride=per), :] = turned

    @pl.when(tm > 0)
    def _():
        forward_gains().wait_recv()

    turned = gather(prior_gains)[count - PRIOR // per : count]
    for j in range(per):
        spread[pl.ds(j, PRIOR // per, stride=per), :] = turned

    for fill in fills:
        fill.wait()

    def place(i):
        far, g = staggered(i // half, groups)
        k = i % half
        return g, k + far * (turned_order(me, k, n) - k)

    def arrive(i):
        g, r = place(i)
        for p in range(len(tails)):

            @pl.when(jnp.logical_and(g == tails[p][0], tm > 0))
            def _():
                forward(p, r).wait_recv()

        for p in range(len(bodies)):

            @pl.when(jnp.logical_and(g == bodies[p][0], r > 0))
            def _():
                send_body(p, r).wait_recv()

    def stream_gains(first):
        rolled = pltpu.roll(spread[...], (LANE - first) % LANE, 1)
        return [jnp.broadcast_to(rolled[:, s : s + 1], rolled.shape) for s in range(width)]

    def segments(i):
        g, r = place(i)
        c, base = xor(r), g * width
        gain = stream_gains(c * own + base)
        streams = []
        for s in range(width):
            raw = jnp.concatenate([tail[c, base + s], got[c, base + s]], axis=0)
            streams.append((raw.astype(jnp.float32) * gain[s]).astype(jnp.bfloat16))
        return jnp.concatenate(streams, axis=1)

    def rotation(i):
        g, r = place(i)
        lane = me * own + g * width
        return chirp(rates[xor(r), lane // 2 % 2, lane // 4])

    def settled():
        @pl.loop(1, n)
        def _(r):
            for send, p in copies[:-1]:
                send(p, r).wait_send()

        @pl.when(has_next)
        def _():
            @pl.loop(0, n)
            def _(r):
                for p in range(len(tails)):
                    forward(p, r).wait_send()

        @pl.loop(1, n)
        def _(r):
            send_gain(r).wait_send()

        @pl.when(has_next)
        def _():
            forward_gains().wait_send()

    @pl.loop(0, items - 1)
    def _(i):
        g, r = place(i)

        @pl.when(i + half < items)
        def _():
            advance(*place(i + half))

        @pl.when(i == items - 2)
        def _():
            settled()

        arrive(i)
        cre, cim = rotation(i)
        result = filtered(segments(i), cre, cim, left, right, unright, back, twist)
        for s in range(width):
            out[g * width + s, xor(r)] = result[:, s * LANE : (s + 1) * LANE]

    late_chirp[0], late_chirp[1] = rotation(items - 1)

    g, r = place(items - 1)
    c, base = xor(r), g * width
    gain = stream_gains(c * own + base)
    for s in range(width):
        cols = slice(s * LANE, (s + 1) * LANE)
        late_gain[:, cols] = gain[s]

    @pl.loop(1, n)
    def _(r):
        send_body(len(bodies) - 1, r).wait_send()

    arrive(items - 1)
    for s in range(width):
        cols = slice(s * LANE, (s + 1) * LANE)
        late[0:PRIOR, cols] = tail[c, base + s]
        late[PRIOR:, cols] = got[c, base + s]


def settle(n, own, width, src, late, late_gain, late_chirp, left, right, unright, back, twist, out, last, bulk_sem, side_sem, last_sem):
    me = lax.axis_index("chan")
    c = bitwise_xor(me, turned_order(me, n // 2 - 1, n), (n - 1).bit_length())
    base = own - width
    bulk = [pltpu.make_async_copy(src.at[q], out.at[q], bulk_sem.at[q]) for q in range(base)]

    def side(s, j):
        peer = (c + j) % n
        return pltpu.make_async_copy(src.at[base + s, peer], out.at[base + s, peer], side_sem.at[s * n + j])

    for copy in bulk:
        copy.start()
    for s in range(width):

        @pl.loop(1, n)
        def _(j):
            side(s, j).start()

    segments = (late[...].astype(jnp.float32) * late_gain[...]).astype(jnp.bfloat16)
    result = filtered(segments, late_chirp[0], late_chirp[1], left, right, unright, back, twist)
    final = []
    for s in range(width):
        last[s] = result[:, s * LANE : (s + 1) * LANE]
        final.append(pltpu.make_async_copy(last.at[s], out.at[base + s, c], last_sem.at[s]))
        final[s].start()
    for s in range(width):

        @pl.loop(1, n)
        def _(j):
            side(s, j).wait()

    for copy in bulk + final:
        copy.wait()


def body(volts, scales, dm_rate):
    lanes, seg_len = volts.shape[1], volts.shape[3]
    count = scales.shape[2]
    n, n_tm = lax.axis_size("chan"), lax.axis_size("tm")
    own = lanes // n
    width = 2 if own % 2 == 0 else 1
    rows = seg_len // LANE * 2
    values = volts.reshape(lanes, 2, seg_len // LANE, LANE).transpose(0, 2, 1, 3).reshape(lanes, rows, LANE)
    consts = tables()
    groups = own // width
    items = n * groups
    early = 2
    vmem = pl.BlockSpec(memory_space=pltpu.VMEM)
    hbm = pl.BlockSpec(memory_space=pltpu.MemorySpace.HBM)
    dma = pltpu.SemaphoreType.DMA
    bf16, f32 = jnp.bfloat16, jnp.float32
    kept = pl.pallas_call(
        functools.partial(kernel, n, n_tm, own, width, early),
        out_shape=[
            pltpu.VMEM((own, n, rows, LANE), bf16),
            pltpu.VMEM((PRIOR + rows, width * LANE), bf16),
            pltpu.VMEM((PRIOR + rows, width * LANE), f32),
            pltpu.VMEM((2, RADIX_A, RADIX_B), f32),
        ]
        + [pltpu.VMEM(x.shape, x.dtype) for x in consts],
        in_specs=[hbm] * 8,
        out_specs=[vmem] * 9,
        scratch_shapes=[
            pltpu.VMEM((n, own, rows, LANE), bf16),
            pltpu.VMEM((n, own, PRIOR, LANE), bf16),
            pltpu.VMEM((n, own, count), f32),
            pltpu.VMEM((n, own, LANE), f32),
            pltpu.VMEM((n, own, LANE), f32),
            pltpu.VMEM((n, own, LANE), f32),
            pltpu.VMEM((LANE, LANE), f32),
            pltpu.VMEM((PRIOR + rows, LANE), f32),
            dma((2,)),
            dma((6,)),
            dma((n,)),
            dma((n,)),
            dma((1,)),
            dma((1,)),
        ]
        + [dma((items,))] * 6
        + [pltpu.SemaphoreType.REGULAR((3,)), pltpu.SMEM((n, 2, lanes // 4), jnp.int32)],
        compiler_params=pltpu.CompilerParams(
            collective_id=0, has_side_effects=True, vmem_limit_bytes=52 * 2**20
        ),
        name="dedisperse",
    )(dm_rate.transpose(0, 2, 1), scales.reshape(n, own, count), values, *consts)
    out = pl.pallas_call(
        functools.partial(settle, n, own, width),
        out_shape=jax.ShapeDtypeStruct((own, n, rows, LANE), bf16),
        in_specs=[vmem] * 9,
        out_specs=hbm,
        scratch_shapes=[
            pltpu.VMEM((width, rows, LANE), bf16),
            dma((max(own - width, 1),)),
            dma((width * n,)),
            dma((width,)),
        ],
        compiler_params=pltpu.CompilerParams(vmem_limit_bytes=16 * 2**20),
        name="settle",
    )(*kept)
    out = out.reshape(own, n, seg_len // LANE, 2, LANE).transpose(0, 1, 3, 2, 4)
    return out.reshape(own, n, 2, seg_len)


def solution(mesh):
    return jax.shard_map(
        body,
        mesh=mesh,
        in_specs=(P("chan", None, None, "tm"), P("chan", None, "tm"), P()),
        out_specs=P("chan", None, None, "tm"),
        check_vma=False,
    )
```

```python
import functools
import math

import jax
import jax.numpy as jnp
import ml_dtypes
import numpy as np
from jax import lax
from jax.experimental import pallas as pl
from jax.experimental.pallas import tpu as pltpu
from jax.sharding import PartitionSpec as P

RADIX_A = 128
RADIX_B = 256
NFFT = RADIX_A * RADIX_B
INTERSECTION = 8192
LANE = 128
HALVES = RADIX_B // LANE
PRIOR = INTERSECTION // LANE * 2
MESH = pl.DeviceIdType.MESH


def dft_parts(radix):
    index = np.arange(radix)
    angle = 2.0 * np.pi / radix * (np.outer(index, index) % radix)
    rounded = lambda x: x.astype(np.float32).astype(ml_dtypes.bfloat16).astype(np.float32)
    return rounded(np.cos(angle)), rounded(-np.sin(angle))


def tables():
    are, aim = dft_parts(RADIX_A)
    bre, bim = dft_parts(RADIX_B)
    eye = np.eye(HALVES, dtype=np.float32)
    left = np.array([[are, -aim], [aim, are]])
    left = np.einsum("dckn,hg->hdkngc", left, eye).reshape(HALVES * 2 * RADIX_A, -1)
    back = np.array([[are, aim], [-aim, are]]) / NFFT
    back = np.einsum("dcnk,hg->nhdgck", back, eye).reshape(-1, HALVES * 2 * RADIX_A)
    back = back[PRIOR:]
    right = np.array([[bre, bim], [-bim, bre]])
    right = right.transpose(0, 2, 1, 3).reshape(2 * RADIX_B, 2 * RADIX_B)
    unright = np.array([[bre, -bim], [bim, bre]])
    unright = unright.transpose(0, 2, 1, 3).reshape(2 * RADIX_B, 2 * RADIX_B)
    turn = np.outer(np.arange(RADIX_A), np.arange(RADIX_B)) % NFFT
    angle = 2.0 * np.pi / NFFT * turn
    twist = np.stack([np.cos(angle), -np.sin(angle)]).astype(np.float32)
    half = lambda x: x.astype(ml_dtypes.bfloat16)
    return half(left), half(right), half(unright), half(back), twist


def chirp(rate):
    shape = (RADIX_A, RADIX_B)
    k = lax.broadcasted_iota(jnp.int32, shape, 0) + RADIX_A * lax.broadcasted_iota(jnp.int32, shape, 1)
    g = jnp.minimum(k, NFFT - k)
    phase = rate * (g * g) - (k << 29)
    quarter = (phase + (1 << 29)) >> 30
    x = (phase - (quarter << 30)).astype(jnp.float32) * (2.0 * math.pi / 2.0**32)
    y = x * x
    s = x + x * y * (-1.6666654611e-1 + y * (8.3321608736e-3 + y * -1.9515295891e-4))
    c = 1.0 + y * (-0.5 + y * (4.166664568298827e-2 + y * (-1.388731625493765e-3 + y * 2.443315711809948e-5)))
    odd = (quarter & 1) == 1
    re = jnp.where(odd, s, c)
    im = jnp.where(odd, c, s)
    re = jnp.where(((quarter + 1) & 2) == 2, -re, re)
    im = jnp.where((quarter & 2) == 2, -im, im)
    return re, im


def filtered(segments, cre, cim, left, right, unright, back, twist):
    wre, wim = twist[0], twist[1]
    section = jnp.dot(left[...], segments, preferred_element_type=jnp.float32)
    ups = []
    for s in range(segments.shape[1] // LANE):
        cols = slice(s * LANE, (s + 1) * LANE)
        part = lambda d: jnp.concatenate(
            [section[(h * 2 + d) * RADIX_A : (h * 2 + d + 1) * RADIX_A, cols] for h in range(HALVES)], axis=1
        )
        sre, sim = part(0), part(1)
        turned = jnp.concatenate(
            [(sre * wre - sim * wim).astype(jnp.bfloat16), (sre * wim + sim * wre).astype(jnp.bfloat16)], axis=1
        )
        spec = jnp.dot(turned, right[...], preferred_element_type=jnp.float32)
        sre, sim = spec[:, :RADIX_B], spec[:, RADIX_B:]
        shaped = jnp.concatenate(
            [(sre * cre - sim * cim).astype(jnp.bfloat16), (sre * cim + sim * cre).astype(jnp.bfloat16)], axis=1
        )
        spun = jnp.dot(shaped, unright[...], preferred_element_type=jnp.float32)
        sre, sim = spun[:, :RADIX_B], spun[:, RADIX_B:]
        ure = (sre * wre + sim * wim).astype(jnp.bfloat16)
        uim = (sim * wre - sre * wim).astype(jnp.bfloat16)
        pieces = []
        for h in range(HALVES):
            pieces += [ure[:, h * LANE : (h + 1) * LANE], uim[:, h * LANE : (h + 1) * LANE]]
        ups.append(jnp.concatenate(pieces, axis=0))
    return jnp.dot(
        back[...], jnp.concatenate(ups, axis=1), preferred_element_type=jnp.float32
    ).astype(jnp.bfloat16)


def bitwise_xor(a, b, bits):
    total = 0
    for i in range(bits):
        total = total + (a // 2**i + b // 2**i) % 2 * 2**i
    return total


def parts(groups):
    if groups > 2:
        return [(0, groups - 2), (groups - 2, 2)], [(g, 1) for g in range(groups)]
    return [(0, groups)], [(g, 1) for g in range(groups)]


def staggered(b, groups):
    last = 2 * groups - 1
    far = 1 - (1 - (b + last) // (last + 1)) - b % 2 + b // last
    return far, (b + 1) // 2 - far


def turned_order(me, k, n):
    half = n // 2
    outer = 1 - (me // half + me // max(half // 2, 1)) % 2
    return half + (k + half // 2 * outer) % half


def kernel(n, n_tm, own, width, early, rates_in, scales, volts, left_in, right_in, unright_in, back_in, twist_in,
           out, late, late_gain, late_chirp, left, right, unright, back, twist,
           got, tail, local_scales, mine, gains, prior_gains, square, spread,
           own_sem, table_sem, gain_send, gain_recv, prior_send, prior_recv, tail_send, tail_recv,
           body_send, body_recv, next_send, next_recv, ready, rates):
    me = lax.axis_index("chan")
    tm = lax.axis_index("tm")
    groups = own // width
    items = n * groups
    half = n // 2
    rows = volts.shape[1]
    count = scales.shape[2]
    bits = (n - 1).bit_length()
    root = n - 1
    across = n - 2
    xor = lambda r: bitwise_xor(me, r, bits)
    has_next = tm < n_tm - 1

    def signal(sem, peer):
        pl.semaphore_signal(sem, inc=1, device_id={"chan": peer}, device_id_type=MESH)

    def remote(src, dst, send, recv, device_id):
        return pltpu.make_async_remote_copy(
            src_ref=src, dst_ref=dst, send_sem=send, recv_sem=recv, device_id=device_id, device_id_type=MESH
        )

    tails, bodies = parts(groups)

    def send_tail(p, r):
        peer = xor(r)
        lane, lanes = tails[p][0] * width, tails[p][1] * width
        cut = pl.ds(rows - PRIOR, PRIOR)
        return remote(
            volts.at[pl.ds(peer * own + lane, lanes), cut], got.at[me, pl.ds(lane, lanes), cut],
            tail_send.at[p * n + r], tail_recv.at[p * n + r], {"chan": peer},
        )

    def send_body(p, r):
        peer = xor(r)
        lane, lanes = bodies[p][0] * width, bodies[p][1] * width
        cut = pl.ds(0, rows - PRIOR)
        return remote(
            volts.at[pl.ds(peer * own + lane, lanes), cut], got.at[me, pl.ds(lane, lanes), cut],
            body_send.at[p * n + r], body_recv.at[p * n + r], {"chan": peer},
        )

    def send_gain(r):
        peer = xor(r)
        return remote(mine.at[peer], gains.at[me], gain_send.at[r], gain_recv.at[r], {"chan": peer})

    def forward_gains():
        return remote(gains, prior_gains, prior_send.at[0], prior_recv.at[0], {"tm": tm + 1})

    def forward(p, r):
        peer = xor(r)
        lanes = pl.ds(tails[p][0] * width, tails[p][1] * width)
        return remote(
            got.at[peer, lanes, pl.ds(rows - PRIOR, PRIOR)], tail.at[peer, lanes],
            next_send.at[p * n + r], next_recv.at[p * n + r], {"tm": tm + 1},
        )

    own_items = pltpu.make_async_copy(volts.at[pl.ds(me * own, own)], got.at[me], own_sem.at[0])
    own_gains = pltpu.make_async_copy(scales, local_scales, own_sem.at[1])
    fills = [
        pltpu.make_async_copy(src, dst, table_sem.at[j])
        for j, (src, dst) in enumerate(
            [(rates_in, rates), (left_in, left), (twist_in, twist), (right_in, right), (unright_in, unright), (back_in, back)]
        )
    ]

    barrier = pltpu.get_barrier_semaphore()
    is_root = me == root
    signal(barrier, xor(across))

    @pl.when(me < root)
    def _():
        signal(barrier, root)

    own_gains.start()
    followed, preceded = 1 - (tm + 1) // n_tm, 1 - (n_tm - tm) // n_tm

    @pl.when(jnp.logical_and(is_root, tm > 0))
    def _():
        pl.semaphore_signal(barrier, inc=1, device_id={"tm": tm - 1}, device_id_type=MESH)

    @pl.when(jnp.logical_and(is_root, has_next))
    def _():
        pl.semaphore_signal(barrier, inc=1, device_id={"tm": tm + 1}, device_id_type=MESH)

    pl.semaphore_wait(barrier, 1 + (me + 1) // n * (n - 1 + followed + preceded))

    def release(k):
        for peer in range(root):
            signal(ready.at[k], peer)

    @pl.when(is_root)
    def _():
        release(0)

    @pl.when(jnp.logical_and(is_root, tm > 0))
    def _():
        pl.semaphore_signal(ready.at[2], inc=1, device_id={"tm": tm - 1}, device_id_type=MESH)

    copies = [(send_tail, 0)] + [(send_body, p) for p in range(len(bodies))]
    copies[3:3] = [(send_tail, p) for p in range(1, len(tails))]

    for send, p in copies[:early]:
        send(p, across).start()

    @pl.when(me < root)
    def _():
        pl.semaphore_wait(ready.at[0], 1)

    for q, (send, p) in enumerate(copies):
        for j in range(1, n):
            r = j % 2 * half + j // 2
            if r != across or q >= early:
                send(p, r).start()
        if q == 0:
            own_gains.wait()
            mine[...] = jnp.zeros_like(mine)
            mine[:, :, 0:count] = local_scales[...]
            for r in range(1, n):
                send_gain(r).start()

    own_items.start()
    for fill in fills:
        fill.start()

    @pl.when(tm == 0)
    def _():
        prior_gains[...] = jnp.zeros_like(prior_gains)

        @pl.loop(0, n)
        def _(c):
            tail[c] = jnp.zeros(tail.shape[1:], tail.dtype)

    @pl.when(jnp.logical_and(is_root, has_next))
    def _():
        pl.semaphore_wait(ready.at[2], 1)

    @pl.when(jnp.logical_and(is_root, has_next))
    def _():
        release(1)

    @pl.when(jnp.logical_and(me < root, has_next))
    def _():
        pl.semaphore_wait(ready.at[1], 1)

    gains[me] = mine[me]

    @pl.loop(1, n)
    def _(r):
        send_gain(r).wait_recv()

    @pl.when(has_next)
    def _():
        forward_gains().start()

    own_items.wait()

    def advance(g, r):
        for p in range(len(tails)):

            @pl.when(jnp.logical_and(g == tails[p][0], r > 0))
            def _():
                send_tail(p, r).wait_recv()

            @pl.when(jnp.logical_and(g == tails[p][0], has_next))
            def _():
                forward(p, r).start()

    @pl.loop(0, half)
    def _(i):
        advance(0, i)

    per = rows // count
    square[...] = jnp.zeros_like(square)

    def gather(src):
        for c in range(n):
            square[c * own : (c + 1) * own] = src[c]
        return square[...].T

    turned = gather(gains)[0:count]
    for j in range(per):
        spread[pl.ds(PRIOR + j, count, stride=per), :] = turned

    @pl.when(tm > 0)
    def _():
        forward_gains().wait_recv()

    turned = gather(prior_gains)[count - PRIOR // per : count]
    for j in range(per):
        spread[pl.ds(j, PRIOR // per, stride=per), :] = turned

    for fill in fills:
        fill.wait()

    def place(i):
        far, g = staggered(i // half, groups)
        k = i % half
        return g, k + far * (turned_order(me, k, n) - k)

    def arrive(i):
        g, r = place(i)
        for p in range(len(tails)):

            @pl.when(jnp.logical_and(g == tails[p][0], tm > 0))
            def _():
                forward(p, r).wait_recv()

        for p in range(len(bodies)):

            @pl.when(jnp.logical_and(g == bodies[p][0], r > 0))
            def _():
                send_body(p, r).wait_recv()

    def stream_gains(first):
        rolled = pltpu.roll(spread[...], (LANE - first) % LANE, 1)
        return [jnp.broadcast_to(rolled[:, s : s + 1], rolled.shape) for s in range(width)]

    def segments(i):
        g, r = place(i)
        c, base = xor(r), g * width
        gain = stream_gains(c * own + base)
        streams = []
        for s in range(width):
            raw = jnp.concatenate([tail[c, base + s], got[c, base + s]], axis=0)
            streams.append((raw.astype(jnp.float32) * gain[s]).astype(jnp.bfloat16))
        return jnp.concatenate(streams, axis=1)

    def rotation(i):
        g, r = place(i)
        lane = me * own + g * width
        return chirp(rates[xor(r), lane // 2 % 2, lane // 4])

    def settled():
        @pl.loop(1, n)
        def _(r):
            for send, p in copies[:-1]:
                send(p, r).wait_send()

        @pl.when(has_next)
        def _():
            @pl.loop(0, n)
            def _(r):
                for p in range(len(tails)):
                    forward(p, r).wait_send()

        @pl.loop(1, n)
        def _(r):
            send_gain(r).wait_send()

        @pl.when(has_next)
        def _():
            forward_gains().wait_send()

    @pl.loop(0, items - 1)
    def _(i):
        g, r = place(i)

        @pl.when(i + half < items)
        def _():
            advance(*place(i + half))

        @pl.when(i == items - 2)
        def _():
            settled()

        arrive(i)
        cre, cim = rotation(i)
        result = filtered(segments(i), cre, cim, left, right, unright, back, twist)
        for s in range(width):
            out[g * width + s, xor(r)] = result[:, s * LANE : (s + 1) * LANE]

    late_chirp[0], late_chirp[1] = rotation(items - 1)

    g, r = place(items - 1)
    c, base = xor(r), g * width
    gain = stream_gains(c * own + base)
    for s in range(width):
        cols = slice(s * LANE, (s + 1) * LANE)
        late_gain[:, cols] = gain[s]

    @pl.loop(1, n)
    def _(r):
        send_body(len(bodies) - 1, r).wait_send()

    arrive(items - 1)
    for s in range(width):
        cols = slice(s * LANE, (s + 1) * LANE)
        late[0:PRIOR, cols] = tail[c, base + s]
        late[PRIOR:, cols] = got[c, base + s]


def settle(n, own, width, src, late, late_gain, late_chirp, left, right, unright, back, twist, out, last, bulk_sem, side_sem, last_sem):
    me = lax.axis_index("chan")
    c = bitwise_xor(me, turned_order(me, n // 2 - 1, n), (n - 1).bit_length())
    base = own - width
    bulk = [pltpu.make_async_copy(src.at[q], out.at[q], bulk_sem.at[q]) for q in range(base)]

    def side(s, j):
        peer = (c + j) % n
        return pltpu.make_async_copy(src.at[base + s, peer], out.at[base + s, peer], side_sem.at[s * n + j])

    for copy in bulk:
        copy.start()
    for s in range(width):

        @pl.loop(1, n)
        def _(j):
            side(s, j).start()

    segments = (late[...].astype(jnp.float32) * late_gain[...]).astype(jnp.bfloat16)
    result = filtered(segments, late_chirp[0], late_chirp[1], left, right, unright, back, twist)
    final = []
    for s in range(width):
        last[s] = result[:, s * LANE : (s + 1) * LANE]
        final.append(pltpu.make_async_copy(last.at[s], out.at[base + s, c], last_sem.at[s]))
        final[s].start()
    for s in range(width):

        @pl.loop(1, n)
        def _(j):
            side(s, j).wait()

    for copy in bulk + final:
        copy.wait()


def body(volts, scales, dm_rate):
    lanes, seg_len = volts.shape[1], volts.shape[3]
    count = scales.shape[2]
    n, n_tm = lax.axis_size("chan"), lax.axis_size("tm")
    own = lanes // n
    width = 2 if own % 2 == 0 else 1
    rows = seg_len // LANE * 2
    values = volts.reshape(lanes, 2, seg_len // LANE, LANE).transpose(0, 2, 1, 3).reshape(lanes, rows, LANE)
    consts = tables()
    groups = own // width
    items = n * groups
    early = 2
    vmem = pl.BlockSpec(memory_space=pltpu.VMEM)
    hbm = pl.BlockSpec(memory_space=pltpu.MemorySpace.HBM)
    dma = pltpu.SemaphoreType.DMA
    bf16, f32 = jnp.bfloat16, jnp.float32
    kept = pl.pallas_call(
        functools.partial(kernel, n, n_tm, own, width, early),
        out_shape=[
            pltpu.VMEM((own, n, rows, LANE), bf16),
            pltpu.VMEM((PRIOR + rows, width * LANE), bf16),
            pltpu.VMEM((PRIOR + rows, width * LANE), f32),
            pltpu.VMEM((2, RADIX_A, RADIX_B), f32),
        ]
        + [pltpu.VMEM(x.shape, x.dtype) for x in consts],
        in_specs=[hbm] * 8,
        out_specs=[vmem] * 9,
        scratch_shapes=[
            pltpu.VMEM((n, own, rows, LANE), bf16),
            pltpu.VMEM((n, own, PRIOR, LANE), bf16),
            pltpu.VMEM((n, own, count), f32),
            pltpu.VMEM((n, own, LANE), f32),
            pltpu.VMEM((n, own, LANE), f32),
            pltpu.VMEM((n, own, LANE), f32),
            pltpu.VMEM((LANE, LANE), f32),
            pltpu.VMEM((PRIOR + rows, LANE), f32),
            dma((2,)),
            dma((6,)),
            dma((n,)),
            dma((n,)),
            dma((1,)),
            dma((1,)),
        ]
        + [dma((items,))] * 6
        + [pltpu.SemaphoreType.REGULAR((3,)), pltpu.SMEM((n, 2, lanes // 4), jnp.int32)],
        compiler_params=pltpu.CompilerParams(
            collective_id=0, has_side_effects=True, vmem_limit_bytes=52 * 2**20
        ),
        name="dedisperse",
    )(dm_rate.transpose(0, 2, 1), scales.reshape(n, own, count), values, *consts)
    out = pl.pallas_call(
        functools.partial(settle, n, own, width),
        out_shape=jax.ShapeDtypeStruct((own, n, rows, LANE), bf16),
        in_specs=[vmem] * 9,
        out_specs=hbm,
        scratch_shapes=[
            pltpu.VMEM((width, rows, LANE), bf16),
            dma((max(own - width, 1),)),
            dma((width * n,)),
            dma((width,)),
        ],
        compiler_params=pltpu.CompilerParams(vmem_limit_bytes=16 * 2**20),
        name="settle",
    )(*kept)
    out = out.reshape(own, n, seg_len // LANE, 2, LANE).transpose(0, 1, 3, 2, 4)
    return out.reshape(own, n, 2, seg_len)


def solution(mesh):
    return jax.shard_map(
        body,
        mesh=mesh,
        in_specs=(P("chan", None, None, "tm"), P("chan", None, "tm"), P()),
        out_specs=P("chan", None, None, "tm"),
        check_vma=False,
    )
```
